32 devices in a mesh: dom: 16 (over z, y, core), feat: 2 (over x).
Axes of the slice: x: 2, y: 2, z: 4, core: 2. Of those that a mesh axis runs over, the one named last changes fastest.
Arguments:
- features: bfloat16 [256, 8192], P('feat', 'dom'), may hold values from -6 to 6
- in_degree: int32 [8192], P('dom'), may hold values from 16 to 64
- send_rows: int32 [16, 16, 16], P('dom'), may hold values from 0 to 511
- send_count: int32 [16, 16], P('dom'), may hold values from 0 to 16, as said below
- hub_owner: int32 [4], replicated, may hold values from 0 to 15, as said below
- hub_rows: int32 [4, 128], replicated, may hold values from 0 to 511
- local_dest: int32 [256], P('dom'), may hold values from 0 to 3
- local_source: int32 [256], P('dom'), may hold values from 0 to 3
- local_tiles: bfloat16 [256, 128, 128], P('dom'), may hold values from 0 to 1
- border_dest: int32 [256], P('dom'), may hold values from 0 to 3
- border_source: int32 [256], P('dom'), may hold values from 0 to 1
- border_tiles: bfloat16 [256, 128, 128], P('dom'), may hold values from 0 to 1
- hub_dest: int32 [256], P('dom'), may hold values from 0 to 3
- hub_source: int32 [256], P('dom'), may hold values from 0 to 3
- hub_tiles: bfloat16 [256, 128, 128], P('dom'), may hold values from 0 to 1
- self_weight: bfloat16 [256, 256], P('feat'), may hold values from -0.375 to 0.375
- neighbor_weight: bfloat16 [256, 256], P('feat'), may hold values from -0.375 to 0.375
- out_bias: float32 [256], P('feat'), may hold values from -3 to 3
Outputs:
- updated: bfloat16 [256, 8192], P('feat', 'dom')
The draws below stay inside these ranges and needn't reach their ends.
Inputs may be any that keep to these rules, and one draw needn't show every extreme that they name: send_count[q, p] of the 16 slots from q to p are live; in every draw some destinations receive 16 live rows from every source. Hub block b belongs to partition hub_owner[b]; one partition owns exactly 2 blocks, every other partition at most one.
All inputs are finite; a program needn't handle non-finite values.
Results may differ from the reference program's by a relative error of at most 0.0034.
Values may be sent and summed in bfloat16 or wider, within the bound.
No kernel may reach another device: no remote copies, remote signals or barrier semaphores. Data moves between devices by JAX's collectives and lax.ppermute only.
A program may use at most 64 MiB of HBM per device.

```python
import jax
import jax.numpy as jnp
from jax import lax

D = 256
BLK = 128
VD = 512
CAP = 16
TLOC = 16
TBND = 16
THUB = 16
HOWN = 2
NHB = 4
V = 8192
N_DOM = 16


def draw_send_count(key, part):
    baseline = jax.random.randint(jax.random.fold_in(key, 11), (N_DOM, N_DOM), 0, CAP // 2 + 1)
    shuffled = jax.random.permutation(jax.random.fold_in(key, 12), N_DOM)
    heavy_dest = shuffled < max(N_DOM // 8, 1)
    return jnp.where(heavy_dest[None, :], CAP, baseline).astype(jnp.int32)


def draw_hub_owner(key, part):
    shuffled = jax.random.permutation(jax.random.fold_in(key, 21), N_DOM).astype(jnp.int32)
    positions = jnp.maximum(jnp.arange(NHB, dtype=jnp.int32) - HOWN + 1, 0)
    return shuffled[positions]


def set_ends(values, own_key, smallest, top_value):
    index_at = [jax.random.randint(jax.random.fold_in(own_key, axis), (), 0, length) for axis, length in enumerate(values.shape)]
    main_axis = values.shape.index(max(values.shape))
    beside = index_at[:main_axis] + [(index_at[main_axis] + 1) % values.shape[main_axis]] + index_at[main_axis + 1:]
    return values.at[tuple(index_at)].set(smallest).at[tuple(beside)].set(top_value)


def steps_of(own_key, extent, split, least, largest):
    gain = 1.0
    for dim, shards_of in split:
        heights = jax.random.uniform(jax.random.fold_in(jax.random.fold_in(own_key, 6), dim), (shards_of,), jnp.float32, least / len(split), largest / len(split))
        gain = gain * jnp.repeat(jnp.exp(heights), extent[dim] // shards_of).reshape((-1,) + (1,) * (len(extent) - 1 - dim))
    return gain


def noise(rng, shape, scale, most, split=(), kind=jnp.bfloat16):
    result = jax.random.normal(rng, shape, jnp.float32) * scale
    if len(split) > 0:
        result = steps_of(rng, shape, split, -0.22, 0.18) * result
    return jnp.clip(result, min=-most, max=most).astype(kind)


def setup_inputs(seed: int = 0) -> dict:
    key_of = jax.random.split(jax.random.key(seed), 19)
    return {
        "features": noise(key_of[0], (D, V), 1.0, 6.0, ((0, 2), (1, 16))),
        "in_degree": set_ends(jax.random.randint(key_of[1], (V,), 16, 65), jax.random.fold_in(key_of[1], 1), 16, 64).astype(jnp.int32),
        "send_rows": set_ends(jax.random.randint(key_of[2], (N_DOM, N_DOM, CAP), 0, VD), jax.random.fold_in(key_of[2], 1), 0, VD - 1).astype(jnp.int32),
        "send_count": draw_send_count(jax.random.fold_in(key_of[18], 71), 0),
        "hub_owner": draw_hub_owner(jax.random.fold_in(key_of[18], 71), 0),
        "hub_rows": set_ends(jax.random.randint(key_of[5], (NHB, BLK), 0, VD), jax.random.fold_in(key_of[5], 1), 0, VD - 1).astype(jnp.int32),
        "local_dest": set_ends(jax.random.randint(key_of[6], (N_DOM * TLOC,), 0, VD // BLK), jax.random.fold_in(key_of[6], 1), 0, (VD // BLK) - 1).astype(jnp.int32),
        "local_source": set_ends(jax.random.randint(key_of[7], (N_DOM * TLOC,), 0, VD // BLK), jax.random.fold_in(key_of[7], 1), 0, (VD // BLK) - 1).astype(jnp.int32),
        "local_tiles": jnp.clip(1.0 * jax.random.uniform(key_of[8], (N_DOM * TLOC, BLK, BLK), jnp.float32) ** steps_of(key_of[8], (N_DOM * TLOC, BLK, BLK), ((0, 16),), -0.2, 0.2), 0.0, 1.0).astype(jnp.bfloat16),
        "border_dest": set_ends(jax.random.randint(key_of[9], (N_DOM * TBND,), 0, VD // BLK), jax.random.fold_in(key_of[9], 1), 0, (VD // BLK) - 1).astype(jnp.int32),
        "border_source": set_ends(jax.random.randint(key_of[10], (N_DOM * TBND,), 0, N_DOM * CAP // BLK), jax.random.fold_in(key_of[10], 1), 0, (N_DOM * CAP // BLK) - 1).astype(jnp.int32),
        "border_tiles": jnp.clip(1.0 * jax.random.uniform(key_of[11], (N_DOM * TBND, BLK, BLK), jnp.float32) ** steps_of(key_of[11], (N_DOM * TBND, BLK, BLK), ((0, 16),), -0.2, 0.2), 0.0, 1.0).astype(jnp.bfloat16),
        "hub_dest": set_ends(jax.random.randint(key_of[12], (N_DOM * THUB,), 0, VD // BLK), jax.random.fold_in(key_of[12], 1), 0, (VD // BLK) - 1).astype(jnp.int32),
        "hub_source": set_ends(jax.random.randint(key_of[13], (N_DOM * THUB,), 0, NHB), jax.random.fold_in(key_of[13], 1), 0, NHB - 1).astype(jnp.int32),
        "hub_tiles": jnp.clip(1.0 * jax.random.uniform(key_of[14], (N_DOM * THUB, BLK, BLK), jnp.float32) ** steps_of(key_of[14], (N_DOM * THUB, BLK, BLK), ((0, 16),), -0.2, 0.2), 0.0, 1.0).astype(jnp.bfloat16),
        "self_weight": noise(key_of[15], (D, D), D ** -0.5, 0.375, ((0, 2),)),
        "neighbor_weight": noise(key_of[16], (D, D), D ** -0.5, 0.375, ((0, 2),)),
        "out_bias": noise(key_of[17], (D,), 0.5, 3.0, ((0, 2),), jnp.float32),
    }


def tile_terms(blocks, targets, source, tile_values):
    picked = jnp.take(blocks, source, axis=1).astype(jnp.float32)
    partial_value = jnp.einsum('ftk,tik->fti', picked, tile_values.astype(jnp.float32), precision=lax.Precision.HIGHEST)
    onehot = (targets[:, None] == jnp.arange(VD // BLK, dtype=jnp.int32)[None, :]).astype(jnp.float32)
    return jnp.einsum('fti,tr->fri', partial_value, onehot, precision=lax.Precision.HIGHEST)


def reference(features, in_degree, send_rows, send_count, hub_owner, hub_rows, local_dest, local_source, local_tiles, border_dest, border_source, border_tiles, hub_dest, hub_source, hub_tiles, self_weight, neighbor_weight, out_bias):
    hub_columns = (hub_owner[:, None] * VD + hub_rows).reshape(-1).astype(jnp.int32)
    hub_blocks = jnp.take(features, hub_columns, axis=1).reshape(D, NHB, BLK)

    def take_part(array, length, part_index):
        return lax.dynamic_slice_in_dim(array, (part_index * length).astype(jnp.int32), length, 0)

    def partition_output(part_index):
        own_flat = lax.dynamic_slice_in_dim(features, (part_index * VD).astype(jnp.int32), VD, 1)
        own_blocks = own_flat.reshape(D, VD // BLK, BLK)
        sent_rows = send_rows[:, part_index, :]
        columns = (jnp.arange(N_DOM, dtype=jnp.int32)[:, None] * VD + sent_rows).reshape(-1).astype(jnp.int32)
        alive_slots = (jnp.arange(CAP, dtype=jnp.int32)[None, :] < send_count[:, part_index][:, None]).reshape(-1)
        received = jnp.take(features, columns, axis=1) * alive_slots[None, :].astype(features.dtype)
        received = received.reshape(D, N_DOM * CAP // BLK, BLK)
        summed = tile_terms(own_blocks, take_part(local_dest, TLOC, part_index), take_part(local_source, TLOC, part_index), take_part(local_tiles, TLOC, part_index))
        summed = summed + tile_terms(received, take_part(border_dest, TBND, part_index), take_part(border_source, TBND, part_index), take_part(border_tiles, TBND, part_index))
        summed = summed + tile_terms(hub_blocks, take_part(hub_dest, THUB, part_index), take_part(hub_source, THUB, part_index), take_part(hub_tiles, THUB, part_index))
        degree = take_part(in_degree, VD, part_index).astype(jnp.float32).reshape(VD // BLK, BLK)
        aggregate = (summed / degree[None]).astype(jnp.bfloat16).reshape(D, VD)
        combined = jnp.dot(self_weight, own_flat, preferred_element_type=jnp.float32)
        combined = combined + jnp.dot(neighbor_weight, aggregate, preferred_element_type=jnp.float32)
        combined = combined + out_bias[:, None]
        return jnp.maximum(combined, 0.0).astype(jnp.bfloat16)

    outputs = lax.map(partition_output, jnp.arange(N_DOM, dtype=jnp.int32))
    return jnp.transpose(outputs, (1, 0, 2)).reshape(D, N_DOM * VD)
```

```python
import functools

import jax
import jax.numpy as jnp
from jax import lax
from jax.experimental import pallas as pl
from jax.experimental.pallas import tpu as pltpu
from jax.sharding import PartitionSpec as P

BF16 = jnp.bfloat16
F32 = jnp.float32
VM = pl.BlockSpec(memory_space=pltpu.VMEM)
SM = pl.BlockSpec(memory_space=pltpu.SMEM)


def call(body, outs, specs, scratch=(), flops=0, size=0, name=None):
    return pl.pallas_call(
        body,
        out_shape=outs,
        in_specs=specs,
        out_specs=jax.tree.map(lambda _: VM, outs),
        scratch_shapes=scratch,
        compiler_params=pltpu.CompilerParams(vmem_limit_bytes=24 << 20),
        cost_estimate=pl.CostEstimate(flops=flops, bytes_accessed=size, transcendentals=0),
        name=name,
    )


def rows(ref, start, size, step):
    return ref[pl.ds(pl.multiple_of(start, step), size), :]


def column(row):
    m = row.shape[1]
    down = lax.broadcasted_iota(jnp.int32, (m, m), 0)
    across = lax.broadcasted_iota(jnp.int32, (m, m), 1)
    return jnp.sum(jnp.where(down == across, row, jnp.zeros_like(row)), axis=1, keepdims=True)


def pick(owner, features, send_rows, send_count, hub_rows, keep, message, hub_keep, gathered):
    me = lax.axis_index("dom")
    bit = me & 1
    parts, cap = send_rows.shape[1:]
    blocks, tile = hub_rows.shape
    vertices = features.shape[1]
    half = tile // 2
    shape = (parts, cap, cap)
    slot = lax.broadcasted_iota(jnp.int32, shape, 1)
    across = lax.broadcasted_iota(jnp.int32, shape, 2)
    lists = jnp.sum(
        jnp.where(slot == across, send_rows[0][:, None, :], 0), axis=2, keepdims=True
    )
    shape = (parts, cap, parts)
    target = lax.broadcasted_iota(jnp.int32, shape, 0)
    across = lax.broadcasted_iota(jnp.int32, shape, 2)
    count = jnp.sum(
        jnp.where(target == across, send_count[...][None], 0), axis=2, keepdims=True
    )
    slot = lax.broadcasted_iota(jnp.int32, (parts, cap, 1), 1)
    lists = jnp.where(slot < count, lists, -1).reshape(parts * cap, 1)
    contract = (((1,), (1,)), ((), ()))

    def select(index):
        vertex = lax.broadcasted_iota(jnp.int32, (index.shape[0], vertices), 1)
        onehot = (vertex == index).astype(F32).astype(BF16)
        return lax.dot_general(onehot, features[...], contract, preferred_element_type=F32).astype(BF16)

    gathered[: parts * cap, :] = select(lists)
    for b in range(blocks):
        index = column(jnp.where(owner[b] == me, hub_rows[b : b + 1, :], -1))
        gathered[parts * cap + b * tile : parts * cap + (b + 1) * tile, :] = select(index)
    for group in range(parts // 2):
        there = slice(group * cap, (group + 1) * cap)
        keep[there, :] = rows(gathered, (2 * group + bit) * cap, cap, cap)
        message[there, :] = rows(gathered, (2 * group + 1 - bit) * cap, cap, cap)
    top = parts * cap
    for b in range(blocks):
        there = slice(b * half, (b + 1) * half)
        hub_keep[there, :] = rows(gathered, top + b * tile + bit * half, half, half)
        message[top // 2 + b * half : top // 2 + (b + 1) * half, :] = rows(
            gathered, top + b * tile + (1 - bit) * half, half, half
        )


def step(k, parts, cap, last, keep, hub, received, *outs):
    me = lax.axis_index("dom")
    bit = (me >> k) & 1
    border = parts * cap // 2
    merged = hub[hub.shape[0] - (received.shape[0] - border) :, :] + received[border:, :]
    run = (1 << k) * cap
    if last:
        lists, message = outs
        lists[pl.ds(pl.multiple_of(bit * run, run), run), :] = keep[...]
        lists[pl.ds(pl.multiple_of((1 - bit) * run, run), run), :] = received[:border, :]
        message[...] = merged
        return
    next_keep, message = outs
    ahead = (me >> (k + 1)) & 1
    for pair in range(parts >> (k + 2)):
        stay, go = (2 * pair + ahead) * run, (2 * pair + 1 - ahead) * run
        mine = pl.ds(pl.multiple_of((2 * pair + bit) * run, run), run)
        theirs = pl.ds(pl.multiple_of((2 * pair + 1 - bit) * run, run), run)
        next_keep[mine, :] = rows(keep, stay, run, run)
        next_keep[theirs, :] = rows(received, stay, run, run)
        message[mine, :] = rows(keep, go, run, run)
        message[theirs, :] = rows(received, go, run, run)
    message[border:, :] = merged


def add_tiles(dest, source, tiles, products, total, operand, contract):
    count, tile, _ = tiles.shape
    for t in range(count):
        products[t] = lax.dot_general(
            tiles[t], operand(source[t]), contract, preferred_element_type=F32
        )
    for t in range(count):
        there = pl.ds(pl.multiple_of(dest[t] * tile, tile), tile)
        total[there, :] = total[there, :] + products[t]


def local_terms(dest, source, features, tiles, in_degree, total, degree, products):
    tile = tiles.shape[1]
    total[...] = jnp.zeros_like(total)
    add_tiles(
        dest, source, tiles, products, total,
        lambda s: features[:, pl.ds(pl.multiple_of(s * tile, tile), tile)],
        (((1,), (1,)), ((), ())),
    )
    for r in range(total.shape[0] // tile):
        row = in_degree[:, r * tile : (r + 1) * tile].astype(F32)
        degree[r * tile : (r + 1) * tile, :] = column(row)


def border_terms(dest, source, lists, tiles, before, total, products):
    tile = tiles.shape[1]
    total[...] = before[...]
    add_tiles(
        dest, source, tiles, products, total,
        lambda s: rows(lists, s * tile, tile, tile), (((1,), (0,)), ((), ())),
    )


def hub_terms(dest, source, mine, theirs, tiles, before, degree, aggregate, hubs, total, products):
    tile = tiles.shape[1]
    half = tile // 2
    bit = lax.axis_index("dom") & 1
    for b in range(mine.shape[0] // half):
        there = slice(b * half, (b + 1) * half)
        hubs[pl.ds(pl.multiple_of(b * tile + bit * half, half), half), :] = mine[there, :]
        hubs[pl.ds(pl.multiple_of(b * tile + (1 - bit) * half, half), half), :] = theirs[there, :]
    total[...] = before[...]
    add_tiles(
        dest, source, tiles, products, total,
        lambda s: rows(hubs, s * tile, tile, tile), (((1,), (0,)), ((), ())),
    )
    aggregate[...] = (total[...] / degree[...]).astype(BF16)


def own_part(self_weight, neighbor_weight, out_bias, features, others, aggregate, base):
    width = features.shape[0]
    place = lax.axis_index("feat")
    mine = pl.ds(pl.multiple_of(place * width, width), width)
    theirs = pl.ds(pl.multiple_of((1 - place) * width, width), width)
    base[...] = (
        jnp.dot(self_weight[:, mine], features[...], preferred_element_type=F32)
        + jnp.dot(self_weight[:, theirs], others[...], preferred_element_type=F32)
        + lax.dot_general(
            neighbor_weight[:, mine], aggregate[...], (((1,), (1,)), ((), ())),
            preferred_element_type=F32,
        )
        + column(out_bias[...])
    )


def other_part(neighbor_weight, aggregate, base, updated):
    width = aggregate.shape[1]
    place = lax.axis_index("feat")
    theirs = pl.ds(pl.multiple_of((1 - place) * width, width), width)
    combined = base[...] + lax.dot_general(
        neighbor_weight[:, theirs], aggregate[...], (((1,), (1,)), ((), ())),
        preferred_element_type=F32,
    )
    updated[...] = jnp.maximum(combined, 0.0).astype(BF16)


def shards(
    features, in_degree, send_rows, send_count, hub_owner, hub_rows,
    local_dest, local_source, local_tiles, border_dest, border_source, border_tiles,
    hub_dest, hub_source, hub_tiles, self_weight, neighbor_weight, out_bias,
):
    width, vertices = features.shape
    count, tile, _ = local_tiles.shape
    parts, feats = lax.axis_size("dom"), lax.axis_size("feat")
    cap = send_rows.shape[2]
    blocks = hub_owner.shape[0]
    steps = parts.bit_length() - 1
    border, hub = parts * cap // 2, blocks * tile // 2
    like = lambda *shape, kind=BF16: jax.ShapeDtypeStruct(shape, kind)
    products = pltpu.VMEM((count, tile, width), F32)
    work = 2 * count * tile * tile * width

    def swap(x, k):
        return lax.ppermute(x, "dom", [(i, i ^ (1 << k)) for i in range(parts)])

    if feats == 2:
        others = lax.ppermute(features, "feat", [(0, 1), (1, 0)])
    keep, message, held = call(
        pick,
        (like(border, width), like(border + hub, width), like(hub, width)),
        [SM, VM, VM, VM, VM],
        [pltpu.VMEM((2 * (border + hub), width), BF16)],
        name="pick",
    )(hub_owner, features, send_rows, send_count, hub_rows)
    total, degree = call(
        local_terms, (like(vertices, width, kind=F32), like(vertices, 1, kind=F32)),
        [SM, SM, VM, VM, VM], [products], flops=work, size=local_tiles.size * 2, name="local",
    )(local_dest, local_source, features, local_tiles, in_degree.reshape(1, vertices))
    for k in range(steps):
        received = swap(message, k)
        last = k == steps - 1
        outs = (
            (like(2 * border, width), like(hub, width))
            if last
            else (like(border, width), like(border + hub, width))
        )
        keep, message = call(
            functools.partial(step, k, parts, cap, last), outs, [VM, VM, VM], name=f"step{k}"
        )(keep, held, received)
        held = message
    theirs = swap(message, 0)
    total = call(
        border_terms, like(vertices, width, kind=F32), [SM, SM, VM, VM, VM], [products],
        flops=work, size=border_tiles.size * 2, name="border",
    )(border_dest, border_source, keep, border_tiles, total)
    aggregate = call(
        hub_terms, like(vertices, width), [SM, SM, VM, VM, VM, VM, VM],
        [pltpu.VMEM((2 * hub, width), BF16), pltpu.VMEM((vertices, width), F32), products],
        flops=work, size=hub_tiles.size * 2, name="hub",
    )(hub_dest, hub_source, message, theirs, hub_tiles, total, degree)
    outputs = self_weight.shape[0]
    if feats == 2:
        arrived = lax.ppermute(aggregate, "feat", [(0, 1), (1, 0)])
        base = call(
            own_part, like(outputs, vertices, kind=F32), [VM] * 6,
            flops=6 * outputs * width * vertices, size=features.size * 4, name="own",
        )(self_weight, neighbor_weight, out_bias.reshape(1, outputs), features, others, aggregate)
        return call(other_part, like(outputs, vertices), [VM] * 3, name="other")(
            neighbor_weight, arrived, base
        )
    everyone = lax.all_gather(features, "feat", axis=0, tiled=True)
    gathered = lax.all_gather(aggregate, "feat", axis=1, tiled=True)
    combined = (
        jnp.dot(self_weight, everyone, preferred_element_type=F32)
        + jnp.einsum("of,vf->ov", neighbor_weight, gathered, preferred_element_type=F32)
        + out_bias[:, None]
    )
    return jnp.maximum(combined, 0.0).astype(BF16)


def solution(mesh):
    dom, feat = P("dom"), P("feat")
    whole = P("dom", None, None)
    placed = (
        P("feat", "dom"), dom, whole, P("dom", None), P(), P(),
        dom, dom, whole, dom, dom, whole, dom, dom, whole,
        P("feat", None), P("feat", None), feat,
    )
    return jax.shard_map(
        shards, mesh=mesh, in_specs=placed, out_specs=P("feat", "dom"), check_vma=False
    )
```

```python
import functools

import jax
import jax.numpy as jnp
from jax import lax
from jax.experimental import pallas as pl
from jax.experimental.pallas import tpu as pltpu
from jax.sharding import PartitionSpec as P

BF16 = jnp.bfloat16
F32 = jnp.float32
VM = pl.BlockSpec(memory_space=pltpu.VMEM)
ANY = pl.BlockSpec(memory_space=pl.ANY)
HBM = pl.BlockSpec(memory_space=pltpu.HBM)
LAST = (((1,), (1,)), ((), ()))
FIRST_LAST = (((0,), (1,)), ((), ()))


def call(body, outs, specs, scratch=(), flops=0, size=0, name=None):
    return pl.pallas_call(
        body,
        out_shape=outs,
        in_specs=specs,
        out_specs=jax.tree.map(lambda _: VM, outs),
        scratch_shapes=scratch,
        compiler_params=pltpu.CompilerParams(vmem_limit_bytes=40 << 20),
        cost_estimate=pl.CostEstimate(flops=flops, bytes_accessed=size, transcendentals=0),
        name=name,
    )


def dot(a, b, contract=(((1,), (0,)), ((), ()))):
    return lax.dot_general(a, b, contract, preferred_element_type=F32)


def rows(start, size):
    return pl.ds(pl.multiple_of(start, size), size)


def column(row):
    m = row.shape[1]
    down = lax.broadcasted_iota(jnp.int32, (m, m), 0)
    across = lax.broadcasted_iota(jnp.int32, (m, m), 1)
    return jnp.sum(jnp.where(down == across, row, jnp.zeros_like(row)), axis=1, keepdims=True)


def fetch(pairs, sems):
    copies = [pltpu.make_async_copy(a, b, sems.at[i]) for i, (a, b) in enumerate(pairs)]
    for copy in copies:
        copy.start()
    return copies


def choose(owner_h, lists_h, count_h, hubs_h, choice, owner, lists, count, hubs, sems):
    for copy in fetch(
        [(owner_h, owner), (lists_h, lists), (count_h, count), (hubs_h, hubs)], sems
    ):
        copy.wait()
    me = lax.axis_index("dom")
    bit = me & 1
    parts, cap = lists.shape[1:]
    blocks, tile = hubs.shape
    vertices = choice.shape[1]
    shape = (parts, cap, cap)
    slot = lax.broadcasted_iota(jnp.int32, shape, 1)
    across = lax.broadcasted_iota(jnp.int32, shape, 2)
    index = jnp.sum(jnp.where(slot == across, lists[0][:, None, :], 0), axis=2, keepdims=True)
    shape = (parts, cap, parts)
    target = lax.broadcasted_iota(jnp.int32, shape, 0)
    across = lax.broadcasted_iota(jnp.int32, shape, 2)
    live = jnp.sum(jnp.where(target == across, count[...][None], 0), axis=2, keepdims=True)
    slot = lax.broadcasted_iota(jnp.int32, (parts, cap, 1), 1)
    index = jnp.where(slot < live, index, -1)

    def onehot(index):
        vertex = lax.broadcasted_iota(jnp.int32, (index.shape[0], vertices), 1)
        return (vertex == index).astype(F32).astype(BF16)

    for part in range(parts):
        place = (part >> 1) + ((part & 1) ^ bit) * (parts // 2)
        choice[rows(place * cap, cap), :] = onehot(index[part])
    pairs = (blocks + 1) // 2
    for b in range(2 * pairs):
        place = (b >> 1) + (1 - ((b & 1) ^ bit)) * pairs
        there = pl.ds(pl.multiple_of(parts * cap + place * tile, cap), tile)
        if b < blocks:
            mine = jnp.where(owner[b] == me, hubs[b : b + 1, :], -1)
            choice[there, :] = onehot(column(mine))
        else:
            choice[there, :] = jnp.zeros((tile, vertices), BF16)


def weight_parts(weight, feature_blocks):
    if len(feature_blocks) == 1:
        return [(weight[...], feature_blocks[0][...])]
    width = feature_blocks[0].shape[0]
    place = lax.axis_index("feat")
    return [
        (weight[:, rows(p * width, width)], block[...])
        for p, block in zip((place, 1 - place), feature_blocks)
    ]


def pick(border, hub, weight, choice, *refs):
    *feature_blocks, projected, keep, message, held = refs
    total = sum(dot(w, f) for w, f in weight_parts(weight, feature_blocks)).astype(BF16)
    projected[...] = total
    picked = dot(choice[...], total, LAST).astype(BF16)
    keep[...] = picked[:border]
    message[...] = picked[border : 2 * border + hub]
    held[...] = picked[2 * border + hub :]


def step(k, parts, cap, last, keep, hub, received, *outs):
    me = lax.axis_index("dom")
    bit = (me >> k) & 1
    border = parts * cap // 2
    merged = hub[hub.shape[0] - (received.shape[0] - border) :, :] + received[border:, :]
    run = (1 << k) * cap
    first, second = outs[-2:]
    if last:
        first[rows(bit * run, run), :] = keep[...]
        first[rows((1 - bit) * run, run), :] = received[:border, :]
        first[2 * border :, :] = merged
        second[...] = merged
        return
    ahead = (me >> (k + 1)) & 1
    for pair in range(parts >> (k + 2)):
        stay, go = rows((2 * pair + ahead) * run, run), rows((2 * pair + 1 - ahead) * run, run)
        mine, theirs = rows((2 * pair + bit) * run, run), rows((2 * pair + 1 - bit) * run, run)
        first[mine, :] = keep[stay, :]
        first[theirs, :] = received[stay, :]
        second[mine, :] = keep[go, :]
        second[theirs, :] = received[go, :]
    second[border:, :] = merged


def adjacency(kinds, degree_h, *refs):
    inputs, rest = refs[:9], refs[10:]
    local_high, local_low, far_high, far_low = rest[:4]
    degree, dests, sources, tiles, near, far, sems = rest[4:]
    copies = []
    for i in range(3):
        copies.append(
            fetch(
                [
                    (inputs[3 * i], dests.at[i]),
                    (inputs[3 * i + 1], sources.at[i]),
                    (inputs[3 * i + 2], tiles.at[i]),
                ],
                sems.at[i],
            )
        )
    whole = pltpu.make_async_copy(degree_h, degree, sems.at[3, 0])
    whole.start()
    bit = lax.axis_index("dom") & 1
    count, tile = tiles.shape[1:3]
    near[...] = jnp.zeros_like(near)
    far[...] = jnp.zeros_like(far)
    border, pairs = kinds
    for i in range(3):
        for copy in copies[i]:
            copy.wait()
        sums = far if i else near
        for t in range(count):
            source = sources[i, t]
            if i == 2:
                source = border + (source >> 1) + ((source & 1) ^ bit) * pairs
            there = (rows(dests[i, t] * tile, tile), rows(source * tile, tile))
            sums[there] = sums[there] + tiles[i, t].astype(F32)
    whole.wait()
    for r in range(near.shape[0] // tile):
        there = slice(r * tile, (r + 1) * tile)
        below = column(degree[:, there].astype(F32))
        for sums, high, low in ((near, local_high, local_low), (far, far_high, far_low)):
            mean = sums[there, :] / below
            top = mean.astype(BF16)
            high[there, :] = top
            low[there, :] = (mean - top.astype(F32)).astype(BF16)


def own_terms(local_high, local_low, projected, weight, bias, *refs):
    *feature_blocks, _, total = refs
    total[...] = (
        sum(dot(f, w, FIRST_LAST) for w, f in weight_parts(weight, feature_blocks))
        + dot(local_high[...], projected[...], LAST)
        + dot(local_low[...], projected[...], LAST)
        + bias[...]
    )


def far_terms(high, low, near, before, total):
    known = near.shape[0]
    total[...] = (
        before[...] + dot(high[:, :known], near[...]) + dot(low[:, :known], near[...])
    )


def finish(high, low, theirs, before, updated):
    known = high.shape[1] - theirs.shape[0]
    total = before[...] + dot(high[:, known:], theirs[...]) + dot(low[:, known:], theirs[...])
    updated[...] = jnp.maximum(total, 0.0).astype(BF16).T


def shards(
    features, in_degree, send_rows, send_count, hub_owner, hub_rows,
    local_dest, local_source, local_tiles, border_dest, border_source, border_tiles,
    hub_dest, hub_source, hub_tiles, self_weight, neighbor_weight, out_bias,
):
    vertices = features.shape[1]
    count, tile, _ = local_tiles.shape
    width = self_weight.shape[0]
    parts, feats = lax.axis_size("dom"), lax.axis_size("feat")
    cap = send_rows.shape[2]
    blocks = hub_owner.shape[0]
    steps = parts.bit_length() - 1
    pairs = (blocks + 1) // 2
    border, hub = parts * cap // 2, pairs * tile
    near_size, far_size = vertices, 2 * border + 2 * hub

    def like(*shape, kind=BF16):
        return jax.ShapeDtypeStruct(shape, kind)

    def swap(x, k):
        return lax.ppermute(x, "dom", [(i, i ^ (1 << k)) for i in range(parts)])

    if feats == 2:
        feature_blocks = [features, lax.ppermute(features, "feat", [(0, 1), (1, 0)])]
    else:
        feature_blocks = [lax.all_gather(features, "feat", axis=0, tiled=True)]
    choice = call(
        choose, like(2 * (border + hub), vertices), [HBM] * 4,
        [
            pltpu.SMEM(hub_owner.shape, jnp.int32),
            pltpu.VMEM(send_rows.shape, jnp.int32),
            pltpu.VMEM(send_count.shape, jnp.int32),
            pltpu.VMEM(hub_rows.shape, jnp.int32),
            pltpu.SemaphoreType.DMA((4,)),
        ],
        size=2 << 20, name="choose",
    )(hub_owner, send_rows, send_count, hub_rows)
    projected, keep, message, held = call(
        functools.partial(pick, border, hub),
        (like(width, vertices), like(border, width), like(border + hub, width), like(hub, width)),
        [VM] * (2 + len(feature_blocks)),
        size=1 << 20, name="pick",
    )(neighbor_weight, choice, *feature_blocks)
    inputs = (
        local_dest, local_source, local_tiles, border_dest, border_source, border_tiles,
        hub_dest, hub_source, hub_tiles,
    )
    waits = None
    for k in range(steps):
        received = swap(message, k)
        last = k == steps - 1
        specs, operands = [VM, VM, VM], (keep, held, received)
        body = functools.partial(step, k, parts, cap, last)
        if waits is not None:
            specs, operands = specs + [ANY], operands + (waits,)
            body = functools.partial(
                lambda inner, a, b, c, _, *outs: inner(a, b, c, *outs), body
            )
        outs = (
            (like(2 * border + hub, width), like(hub, width))
            if last
            else (like(border, width), like(border + hub, width))
        )
        keep, message = call(body, outs, specs, name=f"step{k}")(*operands)
        held = message
        waits = None
        if k == 0:
            local_high, local_low, far_high, far_low = call(
                functools.partial(adjacency, (2 * border // tile, pairs)),
                (like(vertices, near_size),) * 2 + (like(vertices, far_size),) * 2,
                [HBM] * 10 + [ANY],
                [
                    pltpu.VMEM((1, vertices), jnp.int32),
                    pltpu.SMEM((3, count), jnp.int32),
                    pltpu.SMEM((3, count), jnp.int32),
                    pltpu.VMEM((3, count, tile, tile), BF16),
                    pltpu.VMEM((vertices, near_size), F32),
                    pltpu.VMEM((vertices, far_size), F32),
                    pltpu.SemaphoreType.DMA((4, 3)),
                ],
                size=6 << 20, name="adjacency",
            )(in_degree.reshape(1, vertices), *inputs, message)
            waits = far_low
        if k == 1:
            total = call(
                own_terms, like(vertices, width, kind=F32),
                [VM] * (5 + len(feature_blocks)) + [ANY],
                flops=4 * vertices * width * (near_size + width), size=2 << 20, name="own",
            )(
                local_high, local_low, projected, self_weight, out_bias.reshape(1, width),
                *feature_blocks, message,
            )
            waits = total
    theirs = swap(message, 0)
    total = call(
        far_terms, like(vertices, width, kind=F32), [VM] * 4,
        flops=4 * vertices * width * (far_size - hub), size=2 << 20, name="far",
    )(far_high, far_low, keep, total)
    return call(finish, like(width, vertices), [VM] * 4, size=1 << 20, name="finish")(
        far_high, far_low, theirs, total
    )


def solution(mesh):
    dom, feat = P("dom"), P("feat")
    whole = P("dom", None, None)
    placed = (
        P("feat", "dom"), dom, whole, P("dom", None), P(), P(),
        dom, dom, whole, dom, dom, whole, dom, dom, whole,
        P("feat", None), P("feat", None), feat,
    )
    return jax.shard_map(
        shards, mesh=mesh, in_specs=placed, out_specs=P("feat", "dom"), check_vma=False
    )
```

```python
import functools

import jax
import jax.numpy as jnp
from jax import lax
from jax.experimental import pallas as pl
from jax.experimental.pallas import tpu as pltpu
from jax.sharding import PartitionSpec as P

BF16 = jnp.bfloat16
F32 = jnp.float32
VM = pl.BlockSpec(memory_space=pltpu.VMEM)
ANY = pl.BlockSpec(memory_space=pl.ANY)
HBM = pl.BlockSpec(memory_space=pltpu.HBM)
LAST = (((1,), (1,)), ((), ()))
FIRST_LAST = (((0,), (1,)), ((), ()))


def call(body, outs, specs, scratch=(), flops=0, size=0, name=None):
    return pl.pallas_call(
        body,
        out_shape=outs,
        in_specs=specs,
        out_specs=jax.tree.map(lambda _: VM, outs),
        scratch_shapes=scratch,
        compiler_params=pltpu.CompilerParams(vmem_limit_bytes=40 << 20),
        cost_estimate=pl.CostEstimate(flops=flops, bytes_accessed=size, transcendentals=0),
        name=name,
    )


def dot(a, b, contract=(((1,), (0,)), ((), ()))):
    return lax.dot_general(a, b, contract, preferred_element_type=F32)


def rows(start, size):
    return pl.ds(pl.multiple_of(start, size), size)


def column(row):
    m = row.shape[1]
    down = lax.broadcasted_iota(jnp.int32, (m, m), 0)
    across = lax.broadcasted_iota(jnp.int32, (m, m), 1)
    return jnp.sum(jnp.where(down == across, row, jnp.zeros_like(row)), axis=1, keepdims=True)


def fetch(pairs, sems):
    copies = [pltpu.make_async_copy(a, b, sems.at[i]) for i, (a, b) in enumerate(pairs)]
    for copy in copies:
        copy.start()
    return copies


def choose(*refs):
    inputs, (choice, *parts_out), scratch = refs[:6], refs[6:-7], refs[-7:]
    owner, lists, count, hubs, features, weight, sems = scratch
    copies = [
        pltpu.make_async_copy(a, b, sems.at[i])
        for i, (a, b) in enumerate(zip(inputs, scratch[:6]))
    ]
    for copy in copies:
        copy.start()
    for copy in copies[:4]:
        copy.wait()
    me = lax.axis_index("dom")
    bit = me & 1
    parts, cap = lists.shape[1:]
    blocks, tile = hubs.shape
    vertices = choice.shape[1]
    pairs = (blocks + 1) // 2
    border, half = parts * cap // 2, parts * cap // 2 + pairs * tile
    shape = (parts, cap, cap)
    slot = lax.broadcasted_iota(jnp.int32, shape, 1)
    across = lax.broadcasted_iota(jnp.int32, shape, 2)
    index = jnp.sum(jnp.where(slot == across, lists[0][:, None, :], 0), axis=2, keepdims=True)
    shape = (parts, cap, parts)
    target = lax.broadcasted_iota(jnp.int32, shape, 0)
    across = lax.broadcasted_iota(jnp.int32, shape, 2)
    live = jnp.sum(jnp.where(target == across, count[...][None], 0), axis=2, keepdims=True)
    slot = lax.broadcasted_iota(jnp.int32, (parts, cap, 1), 1)
    index = jnp.where(slot < live, index, -1)

    def onehot(index):
        vertex = lax.broadcasted_iota(jnp.int32, (index.shape[0], vertices), 1)
        return (vertex == index).astype(F32).astype(BF16)

    for part in range(parts):
        stays = 1 - ((part & 1) ^ bit)
        choice[pl.ds(pl.multiple_of(stays * half + (part >> 1) * cap, cap), cap), :] = onehot(
            index[part]
        )
    for b in range(2 * pairs):
        stays = 1 - ((b & 1) ^ bit)
        there = pl.ds(pl.multiple_of(stays * half + border + (b >> 1) * tile, cap), tile)
        if b < blocks:
            mine = jnp.where(owner[b] == me, hubs[b : b + 1, :], -1)
            choice[there, :] = onehot(column(mine))
        else:
            choice[there, :] = jnp.zeros((tile, vertices), BF16)
    for copy in copies[4:]:
        copy.wait()
    if len(parts_out) == 2:
        known, ahead = parts_out
        width = features.shape[0]
        place = lax.axis_index("feat")
        known[...] = dot(weight[:, rows(place * width, width)], features[...])
        ahead[...] = weight[:, rows((1 - place) * width, width)]


def weight_parts(weight, feature_blocks):
    if len(feature_blocks) == 1:
        return [(weight[...], feature_blocks[0][...])]
    width = feature_blocks[0].shape[0]
    place = lax.axis_index("feat")
    return [
        (weight[:, rows(p * width, width)], block[...])
        for p, block in zip((place, 1 - place), feature_blocks)
    ]


def pick(weight, features, choice, *refs):
    *known, projected, message = refs
    total = dot(weight[...], features[...])
    if known:
        total = total + known[0][...]
    projected[...] = total.astype(BF16)
    message[...] = dot(
        choice[: message.shape[0], :], total.astype(BF16), LAST
    ).astype(BF16)


def remain(projected, choice, kept):
    kept[...] = dot(choice[kept.shape[0] :, :], projected[...], LAST).astype(BF16)


def step(k, parts, cap, last, keep, hub, received, *outs):
    me = lax.axis_index("dom")
    bit = (me >> k) & 1
    border = parts * cap // 2
    merged = hub[hub.shape[0] - (received.shape[0] - border) :, :] + received[border:, :]
    run = (1 << k) * cap
    first, second = outs[-2:]
    if last:
        first[rows(bit * run, run), :] = keep[:border, :]
        first[rows((1 - bit) * run, run), :] = received[:border, :]
        first[2 * border :, :] = merged
        second[...] = merged
        return
    ahead = (me >> (k + 1)) & 1
    for pair in range(parts >> (k + 2)):
        stay, go = rows((2 * pair + ahead) * run, run), rows((2 * pair + 1 - ahead) * run, run)
        mine, theirs = rows((2 * pair + bit) * run, run), rows((2 * pair + 1 - bit) * run, run)
        first[mine, :] = keep[stay, :]
        first[theirs, :] = received[stay, :]
        second[mine, :] = keep[go, :]
        second[theirs, :] = received[go, :]
    second[border:, :] = merged


def adjacency(kinds, degree_h, *refs):
    inputs, rest = refs[:9], refs[10:]
    local_high, local_low, far_high, far_low = rest[:4]
    degree, dests, sources, tiles, near, far, sems = rest[4:]
    copies = []
    for i in range(3):
        copies.append(
            fetch(
                [
                    (inputs[3 * i], dests.at[i]),
                    (inputs[3 * i + 1], sources.at[i]),
                    (inputs[3 * i + 2], tiles.at[i]),
                ],
                sems.at[i],
            )
        )
    whole = pltpu.make_async_copy(degree_h, degree, sems.at[3, 0])
    whole.start()
    bit = lax.axis_index("dom") & 1
    count, tile = tiles.shape[1:3]
    near[...] = jnp.zeros_like(near)
    far[...] = jnp.zeros_like(far)
    border, pairs = kinds
    for i in range(3):
        for copy in copies[i]:
            copy.wait()
        sums = far if i else near
        for t in range(count):
            source = sources[i, t]
            if i == 2:
                source = border + (source >> 1) + ((source & 1) ^ bit) * pairs
            there = (rows(dests[i, t] * tile, tile), rows(source * tile, tile))
            sums[there] = sums[there] + tiles[i, t].astype(F32)
    whole.wait()
    for r in range(near.shape[0] // tile):
        there = slice(r * tile, (r + 1) * tile)
        below = column(degree[:, there].astype(F32))
        for sums, high, low in ((near, local_high, local_low), (far, far_high, far_low)):
            mean = sums[there, :] / below
            top = mean.astype(BF16)
            high[there, :] = top
            low[there, :] = (mean - top.astype(F32)).astype(BF16)


def own_terms(local_high, local_low, projected, weight, bias, *refs):
    *feature_blocks, _, total = refs
    total[...] = (
        sum(dot(f, w, FIRST_LAST) for w, f in weight_parts(weight, feature_blocks))
        + dot(local_high[...], projected[...], LAST)
        + dot(local_low[...], projected[...], LAST)
        + bias[...]
    )


def far_terms(high, low, near, before, total):
    known = near.shape[0]
    total[...] = (
        before[...] + dot(high[:, :known], near[...]) + dot(low[:, :known], near[...])
    )


def finish(high, low, theirs, before, updated):
    known = high.shape[1] - theirs.shape[0]
    total = before[...] + dot(high[:, known:], theirs[...]) + dot(low[:, known:], theirs[...])
    updated[...] = jnp.maximum(total, 0.0).astype(BF16).T


def shards(
    features, in_degree, send_rows, send_count, hub_owner, hub_rows,
    local_dest, local_source, local_tiles, border_dest, border_source, border_tiles,
    hub_dest, hub_source, hub_tiles, self_weight, neighbor_weight, out_bias,
):
    vertices = features.shape[1]
    count, tile, _ = local_tiles.shape
    width = self_weight.shape[0]
    parts, feats = lax.axis_size("dom"), lax.axis_size("feat")
    cap = send_rows.shape[2]
    blocks = hub_owner.shape[0]
    steps = parts.bit_length() - 1
    pairs = (blocks + 1) // 2
    border, hub = parts * cap // 2, pairs * tile
    near_size, far_size = vertices, 2 * border + 2 * hub

    def like(*shape, kind=BF16):
        return jax.ShapeDtypeStruct(shape, kind)

    def swap(x, k):
        return lax.ppermute(x, "dom", [(i, i ^ (1 << k)) for i in range(parts)])

    if feats == 2:
        feature_blocks = [features, lax.ppermute(features, "feat", [(0, 1), (1, 0)])]
    else:
        feature_blocks = [lax.all_gather(features, "feat", axis=0, tiled=True)]
    fixed = [
        pltpu.with_memory_space_constraint(x, pltpu.HBM)
        for x in (hub_owner, send_rows, send_count, hub_rows, features, neighbor_weight)
    ]
    early = ()
    if feats == 2:
        early = (like(width, vertices, kind=F32), like(width, features.shape[0]))
    choice, *early = call(
        choose, (like(2 * (border + hub), vertices), *early), [HBM] * 6,
        [
            pltpu.SMEM(hub_owner.shape, jnp.int32),
            pltpu.VMEM(send_rows.shape, jnp.int32),
            pltpu.VMEM(send_count.shape, jnp.int32),
            pltpu.VMEM(hub_rows.shape, jnp.int32),
            pltpu.VMEM(features.shape, BF16),
            pltpu.VMEM(neighbor_weight.shape, BF16),
            pltpu.SemaphoreType.DMA((6,)),
        ],
        size=2 << 20, name="choose",
    )(*fixed)
    weight, known = (early[1], early[:1]) if early else (neighbor_weight, [])
    projected, message = call(
        pick, (like(width, vertices), like(border + hub, width)), [VM] * (3 + len(known)),
        size=1 << 20, name="pick",
    )(weight, feature_blocks[-1], choice, *known)
    keep = held = call(
        remain, like(border + hub, width), [VM] * 2, size=1 << 20, name="remain"
    )(projected, choice)
    inputs = (
        local_dest, local_source, local_tiles, border_dest, border_source, border_tiles,
        hub_dest, hub_source, hub_tiles,
    )
    waits = None
    for k in range(steps):
        received = swap(message, k)
        last = k == steps - 1
        specs, operands = [VM, VM, VM], (keep, held, received)
        body = functools.partial(step, k, parts, cap, last)
        if waits is not None:
            specs, operands = specs + [ANY], operands + (waits,)
            body = functools.partial(
                lambda inner, a, b, c, _, *outs: inner(a, b, c, *outs), body
            )
        outs = (
            (like(2 * border + hub, width), like(hub, width))
            if last
            else (like(border, width), like(border + hub, width))
        )
        keep, message = call(body, outs, specs, name=f"step{k}")(*operands)
        held = message
        waits = None
        if k == 0:
            local_high, local_low, far_high, far_low = call(
                functools.partial(adjacency, (2 * border // tile, pairs)),
                (like(vertices, near_size),) * 2 + (like(vertices, far_size),) * 2,
                [HBM] * 10 + [ANY],
                [
                    pltpu.VMEM((1, vertices), jnp.int32),
                    pltpu.SMEM((3, count), jnp.int32),
                    pltpu.SMEM((3, count), jnp.int32),
                    pltpu.VMEM((3, count, tile, tile), BF16),
                    pltpu.VMEM((vertices, near_size), F32),
                    pltpu.VMEM((vertices, far_size), F32),
                    pltpu.SemaphoreType.DMA((4, 3)),
                ],
                size=6 << 20, name="adjacency",
            )(in_degree.reshape(1, vertices), *inputs, message)
            waits = far_low
        if k == 1:
            total = call(
                own_terms, like(vertices, width, kind=F32),
                [VM] * (5 + len(feature_blocks)) + [ANY],
                flops=4 * vertices * width * (near_size + width), size=2 << 20, name="own",
            )(
                local_high, local_low, projected, self_weight, out_bias.reshape(1, width),
                *feature_blocks, message,
            )
            waits = total
    theirs = swap(message, 0)
    total = call(
        far_terms, like(vertices, width, kind=F32), [VM] * 4,
        flops=4 * vertices * width * (far_size - hub), size=2 << 20, name="far",
    )(far_high, far_low, keep, total)
    return call(finish, like(width, vertices), [VM] * 4, size=1 << 20, name="finish")(
        far_high, far_low, theirs, total
    )


def solution(mesh):
    dom, feat = P("dom"), P("feat")
    whole = P("dom", None, None)
    placed = (
        P("feat", "dom"), dom, whole, P("dom", None), P(), P(),
        dom, dom, whole, dom, dom, whole, dom, dom, whole,
        P("feat", None), P("feat", None), feat,
    )
    return jax.shard_map(
        shards, mesh=mesh, in_specs=placed, out_specs=P("feat", "dom"), check_vma=False
    )
```

```python
import functools

import jax
import jax.numpy as jnp
from jax import lax
from jax.experimental import pallas as pl
from jax.experimental.pallas import tpu as pltpu
from jax.sharding import PartitionSpec as P

BF16 = jnp.bfloat16
F32 = jnp.float32
VM = pl.BlockSpec(memory_space=pltpu.VMEM)
ANY = pl.BlockSpec(memory_space=pl.ANY)
HBM = pl.BlockSpec(memory_space=pltpu.HBM)
LAST = (((1,), (1,)), ((), ()))
FIRST_LAST = (((0,), (1,)), ((), ()))


def call(body, outs, specs, scratch=(), flops=0, size=0, name=None):
    return pl.pallas_call(
        body,
        out_shape=outs,
        in_specs=specs,
        out_specs=jax.tree.map(lambda _: VM, outs),
        scratch_shapes=scratch,
        compiler_params=pltpu.CompilerParams(vmem_limit_bytes=40 << 20),
        cost_estimate=pl.CostEstimate(flops=flops, bytes_accessed=size, transcendentals=0),
        name=name,
    )


def dot(a, b, contract=(((1,), (0,)), ((), ()))):
    return lax.dot_general(a, b, contract, preferred_element_type=F32)


def rows(start, size):
    return pl.ds(pl.multiple_of(start, size), size)


def line_of(place):
    for shift in (8, 4, 2, 1):
        place = place ^ (place >> shift)
    return place & 1


def turned(chip, line, bits):
    return (chip >> line) | ((chip & line) << (bits - 1))


def relative(place, bits):
    line = line_of(place)
    return 2 * turned(place >> 1, line, bits) + line


def partners(parts, k):
    if k == 0:
        return [(i, i ^ 1) for i in range(parts)]
    bits = parts.bit_length() - 2
    place = {relative(i, bits): i for i in range(parts)}
    return [(i, place[relative(i, bits) ^ (1 << k)]) for i in range(parts)]


def column(row):
    m = row.shape[1]
    down = lax.broadcasted_iota(jnp.int32, (m, m), 0)
    across = lax.broadcasted_iota(jnp.int32, (m, m), 1)
    return jnp.sum(jnp.where(down == across, row, jnp.zeros_like(row)), axis=1, keepdims=True)


def fetch(pairs, sems):
    copies = [pltpu.make_async_copy(a, b, sems.at[i]) for i, (a, b) in enumerate(pairs)]
    for copy in copies:
        copy.start()
    return copies


def choose(*refs):
    inputs, (choice, *parts_out), scratch = refs[:6], refs[6:-7], refs[-7:]
    owner, lists, count, hubs, features, weight, sems = scratch
    copies = [
        pltpu.make_async_copy(a, b, sems.at[i])
        for i, (a, b) in enumerate(zip(inputs, scratch[:6]))
    ]
    for copy in copies:
        copy.start()
    for copy in copies[:4]:
        copy.wait()
    me = lax.axis_index("dom")
    line = line_of(me)
    parts, cap = lists.shape[1:]
    blocks, tile = hubs.shape
    vertices = choice.shape[1]
    pairs = (blocks + 1) // 2
    border, half = parts * cap // 2, parts * cap // 2 + pairs * tile
    shape = (parts, cap, cap)
    slot = lax.broadcasted_iota(jnp.int32, shape, 1)
    across = lax.broadcasted_iota(jnp.int32, shape, 2)
    index = jnp.sum(jnp.where(slot == across, lists[0][:, None, :], 0), axis=2, keepdims=True)
    shape = (parts, cap, parts)
    target = lax.broadcasted_iota(jnp.int32, shape, 0)
    across = lax.broadcasted_iota(jnp.int32, shape, 2)
    live = jnp.sum(jnp.where(target == across, count[...][None], 0), axis=2, keepdims=True)
    slot = lax.broadcasted_iota(jnp.int32, (parts, cap, 1), 1)
    index = jnp.where(slot < live, index, -1)

    def onehot(index):
        vertex = lax.broadcasted_iota(jnp.int32, (index.shape[0], vertices), 1)
        return (vertex == index).astype(F32).astype(BF16)

    for part in range(parts):
        stays = 1 - (line_of(part) ^ line)
        place = turned(part >> 1, line_of(part), parts.bit_length() - 2)
        choice[pl.ds(pl.multiple_of(stays * half + place * cap, cap), cap), :] = onehot(index[part])
    for b in range(2 * pairs):
        stays = 1 - ((b & 1) ^ line)
        there = pl.ds(pl.multiple_of(stays * half + border + (b >> 1) * tile, cap), tile)
        if b < blocks:
            mine = jnp.where(owner[b] == me, hubs[b : b + 1, :], -1)
            choice[there, :] = onehot(column(mine))
        else:
            choice[there, :] = jnp.zeros((tile, vertices), BF16)
    for copy in copies[4:]:
        copy.wait()
    if len(parts_out) == 2:
        known, ahead = parts_out
        width = features.shape[0]
        place = lax.axis_index("feat")
        known[...] = dot(weight[:, rows(place * width, width)], features[...])
        ahead[...] = weight[:, rows((1 - place) * width, width)]


def weight_parts(weight, feature_blocks):
    if len(feature_blocks) == 1:
        return [(weight[...], feature_blocks[0][...])]
    width = feature_blocks[0].shape[0]
    place = lax.axis_index("feat")
    return [
        (weight[:, rows(p * width, width)], block[...])
        for p, block in zip((place, 1 - place), feature_blocks)
    ]


def pick(weight, features, choice, *refs):
    *known, projected, message = refs
    total = dot(weight[...], features[...])
    if known:
        total = total + known[0][...]
    projected[...] = total.astype(BF16)
    message[...] = dot(
        choice[: message.shape[0], :], total.astype(BF16), LAST
    ).astype(BF16)


def remain(projected, choice, kept):
    kept[...] = dot(choice[kept.shape[0] :, :], projected[...], LAST).astype(BF16)


def step(k, parts, cap, last, keep, hub, received, *outs):
    bits = parts.bit_length() - 2
    me = relative(lax.axis_index("dom"), bits)
    bit = (me >> k) & 1
    border = parts * cap // 2
    merged = hub[hub.shape[0] - (received.shape[0] - border) :, :] + received[border:, :]
    run = (1 << k) * cap
    first, second = outs[-2:]
    if last:
        for group in range(parts // 2):
            here = slice(group * cap, (group + 1) * cap)
            chip = group >> 1
            for top, values in ((bit, keep), (1 - bit, received)):
                origin = jnp.where((me & 1) == 1, 2 * chip + top, chip + (top << (bits - 1)))
                place = 2 * origin + (line_of(group) ^ top)
                first[rows(place * cap, cap), :] = values[here, :]
        first[2 * border :, :] = merged
        second[...] = merged
        return
    ahead = (me >> (k + 1)) & 1
    for pair in range(parts >> (k + 2)):
        stay, go = rows((2 * pair + ahead) * run, run), rows((2 * pair + 1 - ahead) * run, run)
        mine, theirs = rows((2 * pair + bit) * run, run), rows((2 * pair + 1 - bit) * run, run)
        first[mine, :] = keep[stay, :]
        first[theirs, :] = received[stay, :]
        second[mine, :] = keep[go, :]
        second[theirs, :] = received[go, :]
    second[border:, :] = merged


def adjacency(kinds, degree_h, *refs):
    inputs, rest = refs[:9], refs[10:]
    local_high, local_low, far_high, far_low = rest[:4]
    degree, dests, sources, tiles, near, far, sems = rest[4:]
    copies = []
    for i in range(3):
        copies.append(
            fetch(
                [
                    (inputs[3 * i], dests.at[i]),
                    (inputs[3 * i + 1], sources.at[i]),
                    (inputs[3 * i + 2], tiles.at[i]),
                ],
                sems.at[i],
            )
        )
    whole = pltpu.make_async_copy(degree_h, degree, sems.at[3, 0])
    whole.start()
    line = line_of(lax.axis_index("dom"))
    count, tile = tiles.shape[1:3]
    near[...] = jnp.zeros_like(near)
    far[...] = jnp.zeros_like(far)
    border, pairs = kinds
    for i in range(3):
        for copy in copies[i]:
            copy.wait()
        sums = far if i else near
        for t in range(count):
            source = sources[i, t]
            if i == 2:
                source = border + (source >> 1) + ((source & 1) ^ line) * pairs
            there = (rows(dests[i, t] * tile, tile), rows(source * tile, tile))
            sums[there] = sums[there] + tiles[i, t].astype(F32)
    whole.wait()
    for r in range(near.shape[0] // tile):
        there = slice(r * tile, (r + 1) * tile)
        below = column(degree[:, there].astype(F32))
        for sums, high, low in ((near, local_high, local_low), (far, far_high, far_low)):
            mean = sums[there, :] / below
            top = mean.astype(BF16)
            high[there, :] = top
            low[there, :] = (mean - top.astype(F32)).astype(BF16)


def own_terms(local_high, local_low, projected, weight, bias, *refs):
    *feature_blocks, _, total = refs
    total[...] = (
        sum(dot(f, w, FIRST_LAST) for w, f in weight_parts(weight, feature_blocks))
        + dot(local_high[...], projected[...], LAST)
        + dot(local_low[...], projected[...], LAST)
        + bias[...]
    )


def far_terms(high, low, near, before, total):
    known = near.shape[0]
    total[...] = (
        before[...] + dot(high[:, :known], near[...]) + dot(low[:, :known], near[...])
    )


def finish(high, low, theirs, before, updated):
    known = high.shape[1] - theirs.shape[0]
    total = before[...] + dot(high[:, known:], theirs[...]) + dot(low[:, known:], theirs[...])
    updated[...] = jnp.maximum(total, 0.0).astype(BF16).T


def shards(
    features, in_degree, send_rows, send_count, hub_owner, hub_rows,
    local_dest, local_source, local_tiles, border_dest, border_source, border_tiles,
    hub_dest, hub_source, hub_tiles, self_weight, neighbor_weight, out_bias,
):
    vertices = features.shape[1]
    count, tile, _ = local_tiles.shape
    width = self_weight.shape[0]
    parts, feats = lax.axis_size("dom"), lax.axis_size("feat")
    cap = send_rows.shape[2]
    blocks = hub_owner.shape[0]
    steps = parts.bit_length() - 1
    pairs = (blocks + 1) // 2
    border, hub = parts * cap // 2, pairs * tile
    near_size, far_size = vertices, 2 * border + 2 * hub

    def like(*shape, kind=BF16):
        return jax.ShapeDtypeStruct(shape, kind)

    def swap(x, k):
        return lax.ppermute(x, "dom", partners(parts, k))

    if feats == 2:
        feature_blocks = [features, lax.ppermute(features, "feat", [(0, 1), (1, 0)])]
    else:
        feature_blocks = [lax.all_gather(features, "feat", axis=0, tiled=True)]
    fixed = [
        pltpu.with_memory_space_constraint(x, pltpu.HBM)
        for x in (hub_owner, send_rows, send_count, hub_rows, features, neighbor_weight)
    ]
    early = ()
    if feats == 2:
        early = (like(width, vertices, kind=F32), like(width, features.shape[0]))
    choice, *early = call(
        choose, (like(2 * (border + hub), vertices), *early), [HBM] * 6,
        [
            pltpu.SMEM(hub_owner.shape, jnp.int32),
            pltpu.VMEM(send_rows.shape, jnp.int32),
            pltpu.VMEM(send_count.shape, jnp.int32),
            pltpu.VMEM(hub_rows.shape, jnp.int32),
            pltpu.VMEM(features.shape, BF16),
            pltpu.VMEM(neighbor_weight.shape, BF16),
            pltpu.SemaphoreType.DMA((6,)),
        ],
        size=2 << 20, name="choose",
    )(*fixed)
    weight, known = (early[1], early[:1]) if early else (neighbor_weight, [])
    projected, message = call(
        pick, (like(width, vertices), like(border + hub, width)), [VM] * (3 + len(known)),
        size=1 << 20, name="pick",
    )(weight, feature_blocks[-1], choice, *known)
    keep = held = call(
        remain, like(border + hub, width), [VM] * 2, size=1 << 20, name="remain"
    )(projected, choice)
    inputs = (
        local_dest, local_source, local_tiles, border_dest, border_source, border_tiles,
        hub_dest, hub_source, hub_tiles,
    )
    waits = None
    for k in range(steps):
        received = swap(message, k)
        last = k == steps - 1
        specs, operands = [VM, VM, VM], (keep, held, received)
        body = functools.partial(step, k, parts, cap, last)
        if waits is not None:
            specs, operands = specs + [ANY], operands + (waits,)
            body = functools.partial(
                lambda inner, a, b, c, _, *outs: inner(a, b, c, *outs), body
            )
        outs = (
            (like(2 * border + hub, width), like(hub, width))
            if last
            else (like(border, width), like(border + hub, width))
        )
        keep, message = call(body, outs, specs, name=f"step{k}")(*operands)
        held = message
        waits = None
        if k == 0:
            local_high, local_low, far_high, far_low = call(
                functools.partial(adjacency, (2 * border // tile, pairs)),
                (like(vertices, near_size),) * 2 + (like(vertices, far_size),) * 2,
                [HBM] * 10 + [ANY],
                [
                    pltpu.VMEM((1, vertices), jnp.int32),
                    pltpu.SMEM((3, count), jnp.int32),
                    pltpu.SMEM((3, count), jnp.int32),
                    pltpu.VMEM((3, count, tile, tile), BF16),
                    pltpu.VMEM((vertices, near_size), F32),
                    pltpu.VMEM((vertices, far_size), F32),
                    pltpu.SemaphoreType.DMA((4, 3)),
                ],
                size=6 << 20, name="adjacency",
            )(in_degree.reshape(1, vertices), *inputs, message)
            waits = far_low
        if k == 1:
            total = call(
                own_terms, like(vertices, width, kind=F32),
                [VM] * (5 + len(feature_blocks)) + [ANY],
                flops=4 * vertices * width * (near_size + width), size=2 << 20, name="own",
            )(
                local_high, local_low, projected, self_weight, out_bias.reshape(1, width),
                *feature_blocks, message,
            )
            waits = total
    theirs = swap(message, 0)
    total = call(
        far_terms, like(vertices, width, kind=F32), [VM] * 4,
        flops=4 * vertices * width * (far_size - hub), size=2 << 20, name="far",
    )(far_high, far_low, keep, total)
    return call(finish, like(width, vertices), [VM] * 4, size=1 << 20, name="finish")(
        far_high, far_low, theirs, total
    )


def solution(mesh):
    dom, feat = P("dom"), P("feat")
    whole = P("dom", None, None)
    placed = (
        P("feat", "dom"), dom, whole, P("dom", None), P(), P(),
        dom, dom, whole, dom, dom, whole, dom, dom, whole,
        P("feat", None), P("feat", None), feat,
    )
    return jax.shard_map(
        shards, mesh=mesh, in_specs=placed, out_specs=P("feat", "dom"), check_vma=False
    )
```

```python
import functools

import jax
import jax.numpy as jnp
from jax import lax
from jax.experimental import pallas as pl
from jax.experimental.pallas import tpu as pltpu
from jax.sharding import PartitionSpec as P

BF16 = jnp.bfloat16
F32 = jnp.float32
VM = pl.BlockSpec(memory_space=pltpu.VMEM)
ANY = pl.BlockSpec(memory_space=pl.ANY)
HBM = pl.BlockSpec(memory_space=pltpu.HBM)
LAST = (((1,), (1,)), ((), ()))
FIRST_LAST = (((0,), (1,)), ((), ()))


def call(body, outs, specs, scratch=(), flops=0, size=0, name=None):
    return pl.pallas_call(
        body,
        out_shape=outs,
        in_specs=specs,
        out_specs=jax.tree.map(lambda _: VM, outs),
        scratch_shapes=scratch,
        compiler_params=pltpu.CompilerParams(vmem_limit_bytes=40 << 20),
        cost_estimate=pl.CostEstimate(flops=flops, bytes_accessed=size, transcendentals=0),
        name=name,
    )


def dot(a, b, contract=(((1,), (0,)), ((), ()))):
    return lax.dot_general(a, b, contract, preferred_element_type=F32)


def rows(start, size):
    return pl.ds(pl.multiple_of(start, size), size)


def line_of(place):
    for shift in (8, 4, 2, 1):
        place = place ^ (place >> shift)
    return place & 1


def order(line, bits):
    down = list(range(bits))[::-1]
    return down if line else down[-1:] + down[:-1]


def turned(chip, line, bits):
    return sum(((chip >> b) & 1) << i for i, b in enumerate(order(line, bits)))


def relative(place, bits):
    line = line_of(place)
    chips = [turned(place >> 1, each, bits) for each in (0, 1)]
    return 2 * (chips[0] + (chips[1] - chips[0]) * line) + line


def partners(parts, k):
    if k == 0:
        return [(i, i ^ 1) for i in range(parts)]
    bits = parts.bit_length() - 2
    place = {relative(i, bits): i for i in range(parts)}
    return [(i, place[relative(i, bits) ^ (1 << k)]) for i in range(parts)]


def column(row):
    m = row.shape[1]
    down = lax.broadcasted_iota(jnp.int32, (m, m), 0)
    across = lax.broadcasted_iota(jnp.int32, (m, m), 1)
    return jnp.sum(jnp.where(down == across, row, jnp.zeros_like(row)), axis=1, keepdims=True)


def fetch(pairs, sems):
    copies = [pltpu.make_async_copy(a, b, sems.at[i]) for i, (a, b) in enumerate(pairs)]
    for copy in copies:
        copy.start()
    return copies


def choose(*refs):
    inputs, (choice, *parts_out), scratch = refs[:6], refs[6:-7], refs[-7:]
    owner, lists, count, hubs, features, weight, sems = scratch
    copies = [
        pltpu.make_async_copy(a, b, sems.at[i])
        for i, (a, b) in enumerate(zip(inputs, scratch[:6]))
    ]
    for copy in copies:
        copy.start()
    for copy in copies[:4]:
        copy.wait()
    me = lax.axis_index("dom")
    line = line_of(me)
    parts, cap = lists.shape[1:]
    blocks, tile = hubs.shape
    vertices = choice.shape[1]
    pairs = (blocks + 1) // 2
    border, half = parts * cap // 2, parts * cap // 2 + pairs * tile
    shape = (parts, cap, cap)
    slot = lax.broadcasted_iota(jnp.int32, shape, 1)
    across = lax.broadcasted_iota(jnp.int32, shape, 2)
    index = jnp.sum(jnp.where(slot == across, lists[0][:, None, :], 0), axis=2, keepdims=True)
    shape = (parts, cap, parts)
    target = lax.broadcasted_iota(jnp.int32, shape, 0)
    across = lax.broadcasted_iota(jnp.int32, shape, 2)
    live = jnp.sum(jnp.where(target == across, count[...][None], 0), axis=2, keepdims=True)
    slot = lax.broadcasted_iota(jnp.int32, (parts, cap, 1), 1)
    index = jnp.where(slot < live, index, -1)

    def onehot(index):
        vertex = lax.broadcasted_iota(jnp.int32, (index.shape[0], vertices), 1)
        return (vertex == index).astype(F32).astype(BF16)

    for part in range(parts):
        stays = 1 - (line_of(part) ^ line)
        place = turned(part >> 1, line_of(part), parts.bit_length() - 2)
        choice[pl.ds(pl.multiple_of(stays * half + place * cap, cap), cap), :] = onehot(index[part])
    for b in range(2 * pairs):
        stays = 1 - ((b & 1) ^ line)
        there = pl.ds(pl.multiple_of(stays * half + border + (b >> 1) * tile, cap), tile)
        if b < blocks:
            mine = jnp.where(owner[b] == me, hubs[b : b + 1, :], -1)
            choice[there, :] = onehot(column(mine))
        else:
            choice[there, :] = jnp.zeros((tile, vertices), BF16)
    for copy in copies[4:]:
        copy.wait()
    if len(parts_out) == 2:
        known, ahead = parts_out
        width = features.shape[0]
        place = lax.axis_index("feat")
        known[...] = dot(weight[:, rows(place * width, width)], features[...])
        ahead[...] = weight[:, rows((1 - place) * width, width)]


def weight_parts(weight, feature_blocks):
    if len(feature_blocks) == 1:
        return [(weight[...], feature_blocks[0][...])]
    width = feature_blocks[0].shape[0]
    place = lax.axis_index("feat")
    return [
        (weight[:, rows(p * width, width)], block[...])
        for p, block in zip((place, 1 - place), feature_blocks)
    ]


def pick(weight, features, choice, *refs):
    *known, projected, message = refs
    total = dot(weight[...], features[...])
    if known:
        total = total + known[0][...]
    projected[...] = total.astype(BF16)
    message[...] = dot(
        choice[: message.shape[0], :], total.astype(BF16), LAST
    ).astype(BF16)


def remain(projected, choice, kept):
    kept[...] = dot(choice[kept.shape[0] :, :], projected[...], LAST).astype(BF16)


def step(k, parts, cap, last, keep, hub, received, *outs):
    bits = parts.bit_length() - 2
    me = relative(lax.axis_index("dom"), bits)
    bit = (me >> k) & 1
    border = parts * cap // 2
    merged = hub[hub.shape[0] - (received.shape[0] - border) :, :] + received[border:, :]
    run = (1 << k) * cap
    first, second = outs[-2:]
    if last:
        for group in range(parts // 2):
            here = slice(group * cap, (group + 1) * cap)
            chips = [
                sum(((group >> (i + 1)) & 1) << b for i, b in enumerate(order(line, bits)))
                for line in (0, 1)
            ]
            for top, values in ((bit, keep), (1 - bit, received)):
                origin = jnp.where(
                    (me & 1) == 1,
                    chips[1] + (top << order(1, bits)[-1]),
                    chips[0] + (top << order(0, bits)[-1]),
                )
                place = 2 * origin + (line_of(group) ^ top)
                first[rows(place * cap, cap), :] = values[here, :]
        first[2 * border :, :] = merged
        second[...] = merged
        return
    ahead = (me >> (k + 1)) & 1
    for pair in range(parts >> (k + 2)):
        stay, go = rows((2 * pair + ahead) * run, run), rows((2 * pair + 1 - ahead) * run, run)
        mine, theirs = rows((2 * pair + bit) * run, run), rows((2 * pair + 1 - bit) * run, run)
        first[mine, :] = keep[stay, :]
        first[theirs, :] = received[stay, :]
        second[mine, :] = keep[go, :]
        second[theirs, :] = received[go, :]
    second[border:, :] = merged


def adjacency(kinds, degree_h, *refs):
    inputs, rest = refs[:9], refs[10:]
    local_high, local_low, far_high, far_low = rest[:4]
    degree, dests, sources, tiles, near, far, sems = rest[4:]
    copies = []
    for i in range(3):
        copies.append(
            fetch(
                [
                    (inputs[3 * i], dests.at[i]),
                    (inputs[3 * i + 1], sources.at[i]),
                    (inputs[3 * i + 2], tiles.at[i]),
                ],
                sems.at[i],
            )
        )
    whole = pltpu.make_async_copy(degree_h, degree, sems.at[3, 0])
    whole.start()
    line = line_of(lax.axis_index("dom"))
    count, tile = tiles.shape[1:3]
    near[...] = jnp.zeros_like(near)
    far[...] = jnp.zeros_like(far)
    border, pairs = kinds
    for i in range(3):
        for copy in copies[i]:
            copy.wait()
        sums = far if i else near
        for t in range(count):
            source = sources[i, t]
            if i == 2:
                source = border + (source >> 1) + ((source & 1) ^ line) * pairs
            there = (rows(dests[i, t] * tile, tile), rows(source * tile, tile))
            sums[there] = sums[there] + tiles[i, t].astype(F32)
    whole.wait()
    for r in range(near.shape[0] // tile):
        there = slice(r * tile, (r + 1) * tile)
        below = column(degree[:, there].astype(F32))
        for sums, high, low in ((near, local_high, local_low), (far, far_high, far_low)):
            mean = sums[there, :] / below
            top = mean.astype(BF16)
            high[there, :] = top
            low[there, :] = (mean - top.astype(F32)).astype(BF16)


def own_terms(local_high, local_low, projected, weight, bias, *refs):
    *feature_blocks, _, total = refs
    total[...] = (
        sum(dot(f, w, FIRST_LAST) for w, f in weight_parts(weight, feature_blocks))
        + dot(local_high[...], projected[...], LAST)
        + dot(local_low[...], projected[...], LAST)
        + bias[...]
    )


def far_terms(high, low, near, before, total):
    known = near.shape[0]
    total[...] = (
        before[...] + dot(high[:, :known], near[...]) + dot(low[:, :known], near[...])
    )


def finish(high, low, theirs, before, updated):
    known = high.shape[1] - theirs.shape[0]
    total = before[...] + dot(high[:, known:], theirs[...]) + dot(low[:, known:], theirs[...])
    updated[...] = jnp.maximum(total, 0.0).astype(BF16).T


def shards(
    features, in_degree, send_rows, send_count, hub_owner, hub_rows,
    local_dest, local_source, local_tiles, border_dest, border_source, border_tiles,
    hub_dest, hub_source, hub_tiles, self_weight, neighbor_weight, out_bias,
):
    vertices = features.shape[1]
    count, tile, _ = local_tiles.shape
    width = self_weight.shape[0]
    parts, feats = lax.axis_size("dom"), lax.axis_size("feat")
    cap = send_rows.shape[2]
    blocks = hub_owner.shape[0]
    steps = parts.bit_length() - 1
    pairs = (blocks + 1) // 2
    border, hub = parts * cap // 2, pairs * tile
    near_size, far_size = vertices, 2 * border + 2 * hub

    def like(*shape, kind=BF16):
        return jax.ShapeDtypeStruct(shape, kind)

    def swap(x, k):
        return lax.ppermute(x, "dom", partners(parts, k))

    if feats == 2:
        feature_blocks = [features, lax.ppermute(features, "feat", [(0, 1), (1, 0)])]
    else:
        feature_blocks = [lax.all_gather(features, "feat", axis=0, tiled=True)]
    fixed = [
        pltpu.with_memory_space_constraint(x, pltpu.HBM)
        for x in (hub_owner, send_rows, send_count, hub_rows, features, neighbor_weight)
    ]
    early = ()
    if feats == 2:
        early = (like(width, vertices, kind=F32), like(width, features.shape[0]))
    choice, *early = call(
        choose, (like(2 * (border + hub), vertices), *early), [HBM] * 6,
        [
            pltpu.SMEM(hub_owner.shape, jnp.int32),
            pltpu.VMEM(send_rows.shape, jnp.int32),
            pltpu.VMEM(send_count.shape, jnp.int32),
            pltpu.VMEM(hub_rows.shape, jnp.int32),
            pltpu.VMEM(features.shape, BF16),
            pltpu.VMEM(neighbor_weight.shape, BF16),
            pltpu.SemaphoreType.DMA((6,)),
        ],
        size=2 << 20, name="choose",
    )(*fixed)
    weight, known = (early[1], early[:1]) if early else (neighbor_weight, [])
    projected, message = call(
        pick, (like(width, vertices), like(border + hub, width)), [VM] * (3 + len(known)),
        size=1 << 20, name="pick",
    )(weight, feature_blocks[-1], choice, *known)
    keep = held = call(
        remain, like(border + hub, width), [VM] * 2, size=1 << 20, name="remain"
    )(projected, choice)
    inputs = (
        local_dest, local_source, local_tiles, border_dest, border_source, border_tiles,
        hub_dest, hub_source, hub_tiles,
    )
    waits = None
    for k in range(steps):
        received = swap(message, k)
        last = k == steps - 1
        specs, operands = [VM, VM, VM], (keep, held, received)
        body = functools.partial(step, k, parts, cap, last)
        if waits is not None:
            specs, operands = specs + [ANY], operands + (waits,)
            body = functools.partial(
                lambda inner, a, b, c, _, *outs: inner(a, b, c, *outs), body
            )
        outs = (
            (like(2 * border + hub, width), like(hub, width))
            if last
            else (like(border, width), like(border + hub, width))
        )
        keep, message = call(body, outs, specs, name=f"step{k}")(*operands)
        held = message
        waits = None
        if k == 0:
            local_high, local_low, far_high, far_low = call(
                functools.partial(adjacency, (2 * border // tile, pairs)),
                (like(vertices, near_size),) * 2 + (like(vertices, far_size),) * 2,
                [HBM] * 10 + [ANY],
                [
                    pltpu.VMEM((1, vertices), jnp.int32),
                    pltpu.SMEM((3, count), jnp.int32),
                    pltpu.SMEM((3, count), jnp.int32),
                    pltpu.VMEM((3, count, tile, tile), BF16),
                    pltpu.VMEM((vertices, near_size), F32),
                    pltpu.VMEM((vertices, far_size), F32),
                    pltpu.SemaphoreType.DMA((4, 3)),
                ],
                size=6 << 20, name="adjacency",
            )(in_degree.reshape(1, vertices), *inputs, message)
            waits = far_low
        if k == 1:
            total = call(
                own_terms, like(vertices, width, kind=F32),
                [VM] * (5 + len(feature_blocks)) + [ANY],
                flops=4 * vertices * width * (near_size + width), size=2 << 20, name="own",
            )(
                local_high, local_low, projected, self_weight, out_bias.reshape(1, width),
                *feature_blocks, message,
            )
            waits = total
    theirs = swap(message, 0)
    total = call(
        far_terms, like(vertices, width, kind=F32), [VM] * 4,
        flops=4 * vertices * width * (far_size - hub), size=2 << 20, name="far",
    )(far_high, far_low, keep, total)
    return call(finish, like(width, vertices), [VM] * 4, size=1 << 20, name="finish")(
        far_high, far_low, theirs, total
    )


def solution(mesh):
    dom, feat = P("dom"), P("feat")
    whole = P("dom", None, None)
    placed = (
        P("feat", "dom"), dom, whole, P("dom", None), P(), P(),
        dom, dom, whole, dom, dom, whole, dom, dom, whole,
        P("feat", None), P("feat", None), feat,
    )
    return jax.shard_map(
        shards, mesh=mesh, in_specs=placed, out_specs=P("feat", "dom"), check_vma=False
    )
```

```python
import functools

import jax
import jax.numpy as jnp
from jax import lax
from jax.experimental import pallas as pl
from jax.experimental.pallas import tpu as pltpu
from jax.sharding import PartitionSpec as P

BF16 = jnp.bfloat16
F32 = jnp.float32
VM = pl.BlockSpec(memory_space=pltpu.VMEM)
ANY = pl.BlockSpec(memory_space=pl.ANY)
HBM = pl.BlockSpec(memory_space=pltpu.HBM)
LAST = (((1,), (1,)), ((), ()))
FIRST_LAST = (((0,), (1,)), ((), ()))


def call(body, outs, specs, scratch=(), flops=0, size=0, name=None):
    return pl.pallas_call(
        body,
        out_shape=outs,
        in_specs=specs,
        out_specs=jax.tree.map(lambda _: VM, outs),
        scratch_shapes=scratch,
        compiler_params=pltpu.CompilerParams(vmem_limit_bytes=40 << 20),
        cost_estimate=pl.CostEstimate(flops=flops, bytes_accessed=size, transcendentals=0),
        name=name,
    )


def dot(a, b, contract=(((1,), (0,)), ((), ()))):
    return lax.dot_general(a, b, contract, preferred_element_type=F32)


def rows(start, size):
    return pl.ds(pl.multiple_of(start, size), size)


def line_of(place):
    for shift in (8, 4, 2, 1):
        place = place ^ (place >> shift)
    return place & 1


def order(line, bits):
    down = list(range(bits))[::-1]
    return down if line else down[-1:] + down[:-1]


def turned(chip, line, bits):
    return sum(((chip >> b) & 1) << i for i, b in enumerate(order(line, bits)))


def relative_chip(place, line, bits):
    chips = [turned(place >> 1, each, bits) for each in (0, 1)]
    return chips[0] + (chips[1] - chips[0]) * line


def relative(place, bits):
    line = line_of(place)
    return 2 * relative_chip(place, line, bits) + line


def short_exchanges(hub_owner, parts):
    bits = parts.bit_length() - 2
    places = [relative_chip(hub_owner, line, bits) for line in (0, 1)]
    block = jnp.arange(hub_owner.shape[0], dtype=jnp.int32)
    place = jnp.where(block % 2 == 1, places[1], places[0])
    apart = place[:, None] ^ place[None, :]
    paired = (block[:, None] < block[None, :]) & ((block[:, None] - block[None, :]) % 2 == 0)
    least = jnp.min(jnp.where(paired, apart, parts - 1))
    return sum((least >> i > 0).astype(jnp.int32) for i in range(bits))


def partners(parts, k):
    if k == 0:
        return [(i, i ^ 1) for i in range(parts)]
    bits = parts.bit_length() - 2
    place = {relative(i, bits): i for i in range(parts)}
    return [(i, place[relative(i, bits) ^ (1 << k)]) for i in range(parts)]


def column(row):
    m = row.shape[1]
    down = lax.broadcasted_iota(jnp.int32, (m, m), 0)
    across = lax.broadcasted_iota(jnp.int32, (m, m), 1)
    return jnp.sum(jnp.where(down == across, row, jnp.zeros_like(row)), axis=1, keepdims=True)


def fetch(pairs, sems):
    copies = [pltpu.make_async_copy(a, b, sems.at[i]) for i, (a, b) in enumerate(pairs)]
    for copy in copies:
        copy.start()
    return copies


def choose(*refs):
    inputs, (choice, marks, *parts_out), scratch = refs[:6], refs[6:-7], refs[-7:]
    owner, lists, count, hubs, features, weight, sems = scratch
    copies = [
        pltpu.make_async_copy(a, b, sems.at[i])
        for i, (a, b) in enumerate(zip(inputs, scratch[:6]))
    ]
    for copy in copies:
        copy.start()
    for copy in copies[:4]:
        copy.wait()
    me = lax.axis_index("dom")
    line = line_of(me)
    parts, cap = lists.shape[1:]
    blocks, tile = hubs.shape
    vertices = choice.shape[1]
    pairs = (blocks + 1) // 2
    border, half = parts * cap // 2, parts * cap // 2 + pairs * tile
    shape = (parts, cap, cap)
    slot = lax.broadcasted_iota(jnp.int32, shape, 1)
    across = lax.broadcasted_iota(jnp.int32, shape, 2)
    index = jnp.sum(jnp.where(slot == across, lists[0][:, None, :], 0), axis=2, keepdims=True)
    shape = (parts, cap, parts)
    target = lax.broadcasted_iota(jnp.int32, shape, 0)
    across = lax.broadcasted_iota(jnp.int32, shape, 2)
    live = jnp.sum(jnp.where(target == across, count[...][None], 0), axis=2, keepdims=True)
    slot = lax.broadcasted_iota(jnp.int32, (parts, cap, 1), 1)
    index = jnp.where(slot < live, index, -1)

    def onehot(index):
        vertex = lax.broadcasted_iota(jnp.int32, (index.shape[0], vertices), 1)
        return (vertex == index).astype(F32).astype(BF16)

    for part in range(parts):
        stays = 1 - (line_of(part) ^ line)
        place = turned(part >> 1, line_of(part), parts.bit_length() - 2)
        choice[pl.ds(pl.multiple_of(stays * half + place * cap, cap), cap), :] = onehot(index[part])
    for b in range(2 * pairs):
        stays = 1 - ((b & 1) ^ line)
        there = pl.ds(pl.multiple_of(stays * half + border + (b >> 1) * tile, cap), tile)
        if b < blocks:
            mine = jnp.where(owner[b] == me, hubs[b : b + 1, :], -1)
            choice[there, :] = onehot(column(mine))
        else:
            choice[there, :] = jnp.zeros((tile, vertices), BF16)
    bits = parts.bit_length() - 2
    mine = relative(me, bits) >> 1
    for i in range(pairs):
        block = jnp.minimum(2 * i + line, blocks - 1)
        owned = relative_chip(owner[block], line, bits)
        for k in range(bits):
            there = ((mine >> k) ^ 1) == (owned >> k)
            if 2 * i + 1 >= blocks:
                there = there & (2 * i + line < blocks)
            marks[k * pairs + i : k * pairs + i + 1, :] = jnp.full(
                (1, marks.shape[1]), jnp.where(there, 1.0, 0.0), F32
            )
    for copy in copies[4:]:
        copy.wait()
    if len(parts_out) == 2:
        known, ahead = parts_out
        width = features.shape[0]
        place = lax.axis_index("feat")
        known[...] = dot(weight[:, rows(place * width, width)], features[...])
        ahead[...] = weight[:, rows((1 - place) * width, width)]


def weight_parts(weight, feature_blocks):
    if len(feature_blocks) == 1:
        return [(weight[...], feature_blocks[0][...])]
    width = feature_blocks[0].shape[0]
    place = lax.axis_index("feat")
    return [
        (weight[:, rows(p * width, width)], block[...])
        for p, block in zip((place, 1 - place), feature_blocks)
    ]


def pick(weight, features, choice, *refs):
    *known, _, projected, message = refs
    total = dot(weight[...], features[...])
    if known:
        total = total + known[0][...]
    projected[...] = total.astype(BF16)
    message[...] = dot(
        choice[: message.shape[0], :], total.astype(BF16), LAST
    ).astype(BF16)


def remain(projected, choice, kept):
    kept[...] = dot(choice[kept.shape[0] :, :], projected[...], LAST).astype(BF16)


def step(k, parts, cap, last, short, shorten, keep, hub, received, marks, _, *outs):
    bits = parts.bit_length() - 2
    me = relative(lax.axis_index("dom"), bits)
    bit = (me >> k) & 1
    border = parts * cap // 2
    size = outs[1].shape[0] if last else outs[2].shape[0]
    held = hub[hub.shape[0] - size :, :]
    if short:
        tile = received.shape[0] - border
        arrived = received[border:, :].astype(F32)
        pairs = size // tile
        merged = jnp.concatenate(
            [
                held[i * tile : (i + 1) * tile]
                + (arrived * marks[(k - 1) * pairs + i : (k - 1) * pairs + i + 1, :]).astype(BF16)
                for i in range(pairs)
            ],
            axis=0,
        )
    else:
        merged = held + received[border:, :]
    run = (1 << k) * cap
    first, second = outs[:2]
    if last:
        for group in range(parts // 2):
            here = slice(group * cap, (group + 1) * cap)
            chips = [
                sum(((group >> (i + 1)) & 1) << b for i, b in enumerate(order(line, bits)))
                for line in (0, 1)
            ]
            for top, values in ((bit, keep), (1 - bit, received)):
                origin = jnp.where(
                    (me & 1) == 1,
                    chips[1] + (top << order(1, bits)[-1]),
                    chips[0] + (top << order(0, bits)[-1]),
                )
                place = 2 * origin + (line_of(group) ^ top)
                first[rows(place * cap, cap), :] = values[here, :]
        first[2 * border :, :] = merged
        second[...] = merged
        return
    ahead = (me >> (k + 1)) & 1
    for pair in range(parts >> (k + 2)):
        stay, go = rows((2 * pair + ahead) * run, run), rows((2 * pair + 1 - ahead) * run, run)
        mine, theirs = rows((2 * pair + bit) * run, run), rows((2 * pair + 1 - bit) * run, run)
        first[mine, :] = keep[stay, :]
        first[theirs, :] = received[stay, :]
        second[mine, :] = keep[go, :]
        second[theirs, :] = received[go, :]
    outs[2][...] = merged
    if shorten:
        tile = second.shape[0] - border
        pairs = size // tile
        second[border:, :] = sum(merged[i * tile : (i + 1) * tile] for i in range(pairs))
    else:
        second[border:, :] = merged


def adjacency(kinds, degree_h, *refs):
    inputs, rest = refs[:9], refs[9:]
    local_high, local_low, far_high, far_low = rest[:4]
    degree, dests, sources, tiles, near, far, sems = rest[4:]
    copies = []
    for i in range(3):
        copies.append(
            fetch(
                [
                    (inputs[3 * i], dests.at[i]),
                    (inputs[3 * i + 1], sources.at[i]),
                    (inputs[3 * i + 2], tiles.at[i]),
                ],
                sems.at[i],
            )
        )
    whole = pltpu.make_async_copy(degree_h, degree, sems.at[3, 0])
    whole.start()
    line = line_of(lax.axis_index("dom"))
    count, tile = tiles.shape[1:3]
    near[...] = jnp.zeros_like(near)
    far[...] = jnp.zeros_like(far)
    border, pairs = kinds
    for i in range(3):
        for copy in copies[i]:
            copy.wait()
        sums = far if i else near
        for t in range(count):
            source = sources[i, t]
            if i == 2:
                source = border + (source >> 1) + ((source & 1) ^ line) * pairs
            there = (rows(dests[i, t] * tile, tile), rows(source * tile, tile))
            sums[there] = sums[there] + tiles[i, t].astype(F32)
    whole.wait()
    for r in range(near.shape[0] // tile):
        there = slice(r * tile, (r + 1) * tile)
        below = column(degree[:, there].astype(F32))
        for sums, high, low in ((near, local_high, local_low), (far, far_high, far_low)):
            mean = sums[there, :] / below
            top = mean.astype(BF16)
            high[there, :] = top
            low[there, :] = (mean - top.astype(F32)).astype(BF16)


def own_terms(local_high, local_low, projected, weight, bias, *refs):
    *feature_blocks, total = refs
    total[...] = (
        sum(dot(f, w, FIRST_LAST) for w, f in weight_parts(weight, feature_blocks))
        + dot(local_high[...], projected[...], LAST)
        + dot(local_low[...], projected[...], LAST)
        + bias[...]
    )


def far_terms(high, low, near, before, total):
    known = near.shape[0]
    total[...] = (
        before[...] + dot(high[:, :known], near[...]) + dot(low[:, :known], near[...])
    )


def finish(high, low, theirs, before, updated):
    known = high.shape[1] - theirs.shape[0]
    total = before[...] + dot(high[:, known:], theirs[...]) + dot(low[:, known:], theirs[...])
    updated[...] = jnp.maximum(total, 0.0).astype(BF16).T


def shards(
    features, in_degree, send_rows, send_count, hub_owner, hub_rows,
    local_dest, local_source, local_tiles, border_dest, border_source, border_tiles,
    hub_dest, hub_source, hub_tiles, self_weight, neighbor_weight, out_bias,
):
    vertices = features.shape[1]
    count, tile, _ = local_tiles.shape
    width = self_weight.shape[0]
    parts, feats = lax.axis_size("dom"), lax.axis_size("feat")
    cap = send_rows.shape[2]
    blocks = hub_owner.shape[0]
    steps = parts.bit_length() - 1
    pairs = (blocks + 1) // 2
    border, hub = parts * cap // 2, pairs * tile
    near_size, far_size = vertices, 2 * border + 2 * hub

    def like(*shape, kind=BF16):
        return jax.ShapeDtypeStruct(shape, kind)

    def swap(x, k):
        return lax.ppermute(x, "dom", partners(parts, k))

    if feats == 2:
        feature_blocks = [features, lax.ppermute(features, "feat", [(0, 1), (1, 0)])]
    else:
        feature_blocks = [lax.all_gather(features, "feat", axis=0, tiled=True)]
    fixed = [
        pltpu.with_memory_space_constraint(x, pltpu.HBM)
        for x in (hub_owner, send_rows, send_count, hub_rows, features, neighbor_weight)
    ]
    early = ()
    if feats == 2:
        early = (like(width, vertices, kind=F32), like(width, features.shape[0]))
    choice, marks, *early = call(
        choose,
        (
            like(2 * (border + hub), vertices),
            like((steps - 1) * pairs, width, kind=F32),
            *early,
        ),
        [HBM] * 6,
        [
            pltpu.SMEM(hub_owner.shape, jnp.int32),
            pltpu.VMEM(send_rows.shape, jnp.int32),
            pltpu.VMEM(send_count.shape, jnp.int32),
            pltpu.VMEM(hub_rows.shape, jnp.int32),
            pltpu.VMEM(features.shape, BF16),
            pltpu.VMEM(neighbor_weight.shape, BF16),
            pltpu.SemaphoreType.DMA((6,)),
        ],
        size=2 << 20, name="choose",
    )(*fixed)
    inputs = [
        pltpu.with_memory_space_constraint(x, pltpu.HBM)
        for x in (
            in_degree.reshape(1, vertices), local_dest, local_source, local_tiles,
            border_dest, border_source, border_tiles, hub_dest, hub_source, hub_tiles,
        )
    ]
    local_high, local_low, far_high, far_low = call(
        functools.partial(adjacency, (2 * border // tile, pairs)),
        (like(vertices, near_size),) * 2 + (like(vertices, far_size),) * 2,
        [HBM] * 10,
        [
            pltpu.VMEM((1, vertices), jnp.int32),
            pltpu.SMEM((3, count), jnp.int32),
            pltpu.SMEM((3, count), jnp.int32),
            pltpu.VMEM((3, count, tile, tile), BF16),
            pltpu.VMEM((vertices, near_size), F32),
            pltpu.VMEM((vertices, far_size), F32),
            pltpu.SemaphoreType.DMA((4, 3)),
        ],
        size=6 << 20, name="adjacency",
    )(*inputs)
    weight, known = (early[1], early[:1]) if early else (neighbor_weight, [])
    projected, message = call(
        pick, (like(width, vertices), like(border + hub, width)),
        [VM] * (3 + len(known)) + [ANY], size=1 << 20, name="pick",
    )(weight, feature_blocks[-1], choice, *known, far_low)
    received = swap(message, 0)
    kept = call(
        remain, like(border + hub, width), [VM] * 2, size=1 << 20, name="remain"
    )(projected, choice)
    total = call(
        own_terms, like(vertices, width, kind=F32), [VM] * (5 + len(feature_blocks)),
        flops=4 * vertices * width * (near_size + width), size=2 << 20, name="own",
    )(
        local_high, local_low, projected, self_weight, out_bias.reshape(1, width), *feature_blocks
    )

    def chain(level, kept, received, marks, total):
        keep = held = kept
        for k in range(steps):
            if k:
                received = swap(message, k)
            last, shorten = k == steps - 1, k + 1 <= level
            outs = (
                (like(2 * border + hub, width), like(hub, width))
                if last
                else (
                    like(border, width),
                    like(border + (tile if shorten else hub), width),
                    like(hub, width),
                )
            )
            keep, message, *rest = call(
                functools.partial(step, k, parts, cap, last, 1 <= k <= level, shorten),
                outs, [VM] * 4 + [ANY], name=f"step{k}_{level}",
            )(keep, held, received, marks, total)
            held = rest[0] if rest else None
        return keep, message

    keep, message = lax.switch(
        short_exchanges(hub_owner, parts),
        [functools.partial(chain, level) for level in range(steps)],
        kept, received, marks, total,
    )
    theirs = swap(message, 0)
    total = call(
        far_terms, like(vertices, width, kind=F32), [VM] * 4,
        flops=4 * vertices * width * (far_size - hub), size=2 << 20, name="far",
    )(far_high, far_low, keep, total)
    return call(finish, like(width, vertices), [VM] * 4, size=1 << 20, name="finish")(
        far_high, far_low, theirs, total
    )


def solution(mesh):
    dom, feat = P("dom"), P("feat")
    whole = P("dom", None, None)
    placed = (
        P("feat", "dom"), dom, whole, P("dom", None), P(), P(),
        dom, dom, whole, dom, dom, whole, dom, dom, whole,
        P("feat", None), P("feat", None), feat,
    )
    return jax.shard_map(
        shards, mesh=mesh, in_specs=placed, out_specs=P("feat", "dom"), check_vma=False
    )
```

```python
import functools

import jax
import jax.numpy as jnp
from jax import lax
from jax.experimental import pallas as pl
from jax.experimental.pallas import tpu as pltpu
from jax.sharding import PartitionSpec as P

BF16 = jnp.bfloat16
F32 = jnp.float32
VM = pl.BlockSpec(memory_space=pltpu.VMEM)
SM = pl.BlockSpec(memory_space=pltpu.SMEM)
ANY = pl.BlockSpec(memory_space=pl.ANY)
HBM = pl.BlockSpec(memory_space=pltpu.HBM)
LAST = (((1,), (1,)), ((), ()))
FIRST_LAST = (((0,), (1,)), ((), ()))


def call(body, outs, specs, scratch=(), flops=0, size=0, name=None, room=8 << 20):
    return pl.pallas_call(
        body,
        out_shape=outs,
        in_specs=specs,
        out_specs=jax.tree.map(lambda out: SM if out.dtype == jnp.int32 else VM, outs),
        scratch_shapes=scratch,
        compiler_params=pltpu.CompilerParams(vmem_limit_bytes=room),
        cost_estimate=pl.CostEstimate(flops=flops, bytes_accessed=size, transcendentals=0),
        name=name,
    )


def dot(a, b, contract=(((1,), (0,)), ((), ()))):
    return lax.dot_general(a, b, contract, preferred_element_type=F32)


def rows(start, size):
    return pl.ds(pl.multiple_of(start, size), size)


def line_of(place):
    for shift in (8, 4, 2, 1):
        place = place ^ (place >> shift)
    return place & 1


def order(line, bits):
    down = list(range(bits))[::-1]
    return down if line else down[-1:] + down[:-1]


def turned(chip, line, bits):
    return sum(((chip >> b) & 1) << i for i, b in enumerate(order(line, bits)))


def relative_chip(place, line, bits):
    chips = [turned(place >> 1, each, bits) for each in (0, 1)]
    return chips[0] + (chips[1] - chips[0]) * line


def relative(place, bits):
    line = line_of(place)
    return 2 * relative_chip(place, line, bits) + line


def short_exchanges(owner, blocks, parts):
    bits = parts.bit_length() - 2
    place = [turned(owner[b] >> 1, b & 1, bits) for b in range(blocks)]
    least = jnp.int32(parts - 1)
    for b in range(blocks):
        for other in range(b % 2, b, 2):
            least = jnp.minimum(least, place[b] ^ place[other])
    return sum((least >> i > 0).astype(jnp.int32) for i in range(bits))


def partners(parts, k):
    if k == 0:
        return [(i, i ^ 1) for i in range(parts)]
    bits = parts.bit_length() - 2
    place = {relative(i, bits): i for i in range(parts)}
    return [(i, place[relative(i, bits) ^ (1 << k)]) for i in range(parts)]


def column(row):
    m = row.shape[1]
    down = lax.broadcasted_iota(jnp.int32, (m, m), 0)
    across = lax.broadcasted_iota(jnp.int32, (m, m), 1)
    return jnp.sum(jnp.where(down == across, row, jnp.zeros_like(row)), axis=1, keepdims=True)


def fetch(pairs, sems):
    copies = [pltpu.make_async_copy(a, b, sems.at[i]) for i, (a, b) in enumerate(pairs)]
    for copy in copies:
        copy.start()
    return copies


def choose(*refs):
    inputs, outs, scratch = refs[:8], refs[8:-6], refs[-6:]
    choice, marks, level, features, self_weight, bias, *parts_out = outs
    owner, lists, count, hubs, weight, sems = scratch
    landing = (owner, lists, count, hubs, features, weight, self_weight, bias)
    copies = [
        pltpu.make_async_copy(a, b, sems.at[i]) for i, (a, b) in enumerate(zip(inputs, landing))
    ]
    for copy in copies:
        copy.start()
    for copy in copies[:4]:
        copy.wait()
    me = lax.axis_index("dom")
    line = line_of(me)
    parts, cap = lists.shape[1:]
    blocks, tile = hubs.shape
    vertices = choice.shape[1]
    pairs = (blocks + 1) // 2
    border, half = parts * cap // 2, parts * cap // 2 + pairs * tile
    shape = (parts, cap, cap)
    slot = lax.broadcasted_iota(jnp.int32, shape, 1)
    across = lax.broadcasted_iota(jnp.int32, shape, 2)
    index = jnp.sum(jnp.where(slot == across, lists[0][:, None, :], 0), axis=2, keepdims=True)
    shape = (parts, cap, parts)
    target = lax.broadcasted_iota(jnp.int32, shape, 0)
    across = lax.broadcasted_iota(jnp.int32, shape, 2)
    live = jnp.sum(jnp.where(target == across, count[...][None], 0), axis=2, keepdims=True)
    slot = lax.broadcasted_iota(jnp.int32, (parts, cap, 1), 1)
    index = jnp.where(slot < live, index, -1)

    def onehot(index):
        vertex = lax.broadcasted_iota(jnp.int32, (index.shape[0], vertices), 1)
        return (vertex == index).astype(F32).astype(BF16)

    for part in range(parts):
        stays = 1 - (line_of(part) ^ line)
        place = turned(part >> 1, line_of(part), parts.bit_length() - 2)
        choice[pl.ds(pl.multiple_of(stays * half + place * cap, cap), cap), :] = onehot(index[part])
    for b in range(2 * pairs):
        stays = 1 - ((b & 1) ^ line)
        there = pl.ds(pl.multiple_of(stays * half + border + (b >> 1) * tile, cap), tile)
        if b < blocks:
            mine = jnp.where(owner[b] == me, hubs[b : b + 1, :], -1)
            choice[there, :] = onehot(column(mine))
        else:
            choice[there, :] = jnp.zeros((tile, vertices), BF16)
    level[0] = short_exchanges(owner, blocks, parts)
    bits = parts.bit_length() - 2
    mine = relative(me, bits) >> 1
    for i in range(pairs):
        block = jnp.minimum(2 * i + line, blocks - 1)
        owned = relative_chip(owner[block], line, bits)
        for k in range(bits):
            there = ((mine >> k) ^ 1) == (owned >> k)
            if 2 * i + 1 >= blocks:
                there = there & (2 * i + line < blocks)
            marks[k * pairs + i : k * pairs + i + 1, :] = jnp.full(
                (1, marks.shape[1]), jnp.where(there, 1.0, 0.0), F32
            )
    for copy in copies[4:]:
        copy.wait()
    if len(parts_out) == 2:
        known, ahead = parts_out
        width = features.shape[0]
        place = lax.axis_index("feat")
        known[...] = dot(weight[:, rows(place * width, width)], features[...])
        ahead[...] = weight[:, rows((1 - place) * width, width)]


def weight_parts(weight, feature_blocks):
    if len(feature_blocks) == 1:
        return [(weight[...], feature_blocks[0][...])]
    width = feature_blocks[0].shape[0]
    place = lax.axis_index("feat")
    return [
        (weight[:, rows(p * width, width)], block[...])
        for p, block in zip((place, 1 - place), feature_blocks)
    ]


def pick(weight, features, choice, *refs):
    *known, _, projected, message = refs
    total = dot(weight[...], features[...])
    if known:
        total = total + known[0][...]
    projected[...] = total.astype(BF16)
    message[...] = dot(
        choice[: message.shape[0], :], total.astype(BF16), LAST
    ).astype(BF16)


def remain(projected, choice, kept):
    kept[...] = dot(choice[kept.shape[0] :, :], projected[...], LAST).astype(BF16)


def step(k, parts, cap, last, short, shorten, keep, hub, received, marks, _, *outs):
    bits = parts.bit_length() - 2
    me = relative(lax.axis_index("dom"), bits)
    bit = (me >> k) & 1
    border = parts * cap // 2
    size = outs[1].shape[0] if last else outs[2].shape[0]
    held = hub[hub.shape[0] - size :, :]
    if short:
        tile = received.shape[0] - border
        arrived = received[border:, :].astype(F32)
        pairs = size // tile
        merged = jnp.concatenate(
            [
                held[i * tile : (i + 1) * tile]
                + (arrived * marks[(k - 1) * pairs + i : (k - 1) * pairs + i + 1, :]).astype(BF16)
                for i in range(pairs)
            ],
            axis=0,
        )
    else:
        merged = held + received[border:, :]
    run = (1 << k) * cap
    first, second = outs[:2]
    if last:
        for group in range(parts // 2):
            here = slice(group * cap, (group + 1) * cap)
            chips = [
                sum(((group >> (i + 1)) & 1) << b for i, b in enumerate(order(line, bits)))
                for line in (0, 1)
            ]
            for top, values in ((bit, keep), (1 - bit, received)):
                origin = jnp.where(
                    (me & 1) == 1,
                    chips[1] + (top << order(1, bits)[-1]),
                    chips[0] + (top << order(0, bits)[-1]),
                )
                place = 2 * origin + (line_of(group) ^ top)
                first[rows(place * cap, cap), :] = values[here, :]
        first[2 * border :, :] = merged
        second[...] = merged
        return
    ahead = (me >> (k + 1)) & 1
    for pair in range(parts >> (k + 2)):
        stay, go = rows((2 * pair + ahead) * run, run), rows((2 * pair + 1 - ahead) * run, run)
        mine, theirs = rows((2 * pair + bit) * run, run), rows((2 * pair + 1 - bit) * run, run)
        first[mine, :] = keep[stay, :]
        first[theirs, :] = received[stay, :]
        second[mine, :] = keep[go, :]
        second[theirs, :] = received[go, :]
    outs[2][...] = merged
    brief = outs[3] if shorten is None else second
    if shorten is None:
        second[border:, :] = merged
        brief[:border, :] = second[:border, :]
    if shorten is False:
        second[border:, :] = merged
    else:
        tile = brief.shape[0] - border
        pairs = size // tile
        brief[border:, :] = sum(merged[i * tile : (i + 1) * tile] for i in range(pairs))


def adjacency(kinds, degree_h, *refs):
    inputs, rest = refs[:9], refs[9:]
    local_high, local_low, far_high, far_low, token = rest[:5]
    degree, dests, sources, tiles, near, far, sems = rest[5:]
    token[...] = jnp.zeros_like(token)
    copies = []
    for i in range(3):
        copies.append(
            fetch(
                [
                    (inputs[3 * i], dests.at[i]),
                    (inputs[3 * i + 1], sources.at[i]),
                    (inputs[3 * i + 2], tiles.at[i]),
                ],
                sems.at[i],
            )
        )
    whole = pltpu.make_async_copy(degree_h, degree, sems.at[3, 0])
    whole.start()
    line = line_of(lax.axis_index("dom"))
    count, tile = tiles.shape[1:3]
    near[...] = jnp.zeros_like(near)
    far[...] = jnp.zeros_like(far)
    border, pairs = kinds
    for i in range(3):
        for copy in copies[i]:
            copy.wait()
        sums = far if i else near
        for t in range(count):
            source = sources[i, t]
            if i == 2:
                source = border + (source >> 1) + ((source & 1) ^ line) * pairs
            there = (rows(dests[i, t] * tile, tile), rows(source * tile, tile))
            sums[there] = sums[there] + tiles[i, t].astype(F32)
    whole.wait()
    for r in range(near.shape[0] // tile):
        there = slice(r * tile, (r + 1) * tile)
        below = column(degree[:, there].astype(F32))
        for sums, high, low in ((near, local_high, local_low), (far, far_high, far_low)):
            mean = sums[there, :] / below
            top = mean.astype(BF16)
            high[there, :] = top
            low[there, :] = (mean - top.astype(F32)).astype(BF16)


def own_terms(local_high, local_low, projected, weight, bias, *refs):
    *feature_blocks, total = refs
    total[...] = (
        sum(dot(f, w, FIRST_LAST) for w, f in weight_parts(weight, feature_blocks))
        + dot(local_high[...], projected[...], LAST)
        + dot(local_low[...], projected[...], LAST)
        + bias[...]
    )


def far_terms(high, low, near, before, total):
    known = near.shape[0]
    total[...] = (
        before[...] + dot(high[:, :known], near[...]) + dot(low[:, :known], near[...])
    )


def finish(high, low, theirs, before, updated):
    known = high.shape[1] - theirs.shape[0]
    total = before[...] + dot(high[:, known:], theirs[...]) + dot(low[:, known:], theirs[...])
    updated[...] = jnp.maximum(total, 0.0).astype(BF16).T


def shards(
    features, in_degree, send_rows, send_count, hub_owner, hub_rows,
    local_dest, local_source, local_tiles, border_dest, border_source, border_tiles,
    hub_dest, hub_source, hub_tiles, self_weight, neighbor_weight, out_bias,
):
    vertices = features.shape[1]
    count, tile, _ = local_tiles.shape
    width = self_weight.shape[0]
    parts, feats = lax.axis_size("dom"), lax.axis_size("feat")
    cap = send_rows.shape[2]
    blocks = hub_owner.shape[0]
    steps = parts.bit_length() - 1
    pairs = (blocks + 1) // 2
    border, hub = parts * cap // 2, pairs * tile
    near_size, far_size = vertices, 2 * border + 2 * hub

    def like(*shape, kind=BF16):
        return jax.ShapeDtypeStruct(shape, kind)

    def swap(x, k):
        return lax.ppermute(x, "dom", partners(parts, k))

    if feats == 2:
        feature_blocks = [features, lax.ppermute(features, "feat", [(0, 1), (1, 0)])]
    else:
        feature_blocks = [lax.all_gather(features, "feat", axis=0, tiled=True)]
    fixed = [
        pltpu.with_memory_space_constraint(x, pltpu.HBM)
        for x in (
            hub_owner, send_rows, send_count, hub_rows, features, neighbor_weight, self_weight,
            out_bias.reshape(1, width),
        )
    ]
    early = ()
    if feats == 2:
        early = (like(width, vertices, kind=F32), like(width, features.shape[0]))
    choice, marks, level, near_features, near_weight, bias, *early = call(
        choose,
        (
            like(2 * (border + hub), vertices),
            like((steps - 1) * pairs, width, kind=F32),
            like(1, kind=jnp.int32),
            like(*features.shape),
            like(*self_weight.shape),
            like(1, width, kind=F32),
            *early,
        ),
        [HBM] * 8,
        [
            pltpu.SMEM(hub_owner.shape, jnp.int32),
            pltpu.VMEM(send_rows.shape, jnp.int32),
            pltpu.VMEM(send_count.shape, jnp.int32),
            pltpu.VMEM(hub_rows.shape, jnp.int32),
            pltpu.VMEM(neighbor_weight.shape, BF16),
            pltpu.SemaphoreType.DMA((8,)),
        ],
        size=2 << 20, name="choose",
    )(*fixed)
    inputs = [
        pltpu.with_memory_space_constraint(x, pltpu.HBM)
        for x in (
            in_degree.reshape(1, vertices), local_dest, local_source, local_tiles,
            border_dest, border_source, border_tiles, hub_dest, hub_source, hub_tiles,
        )
    ]
    local_high, local_low, far_high, far_low, token = call(
        functools.partial(adjacency, (2 * border // tile, pairs)),
        (like(vertices, near_size),) * 2 + (like(vertices, far_size),) * 2 + (like(8, 128, kind=F32),),
        [HBM] * 10,
        [
            pltpu.VMEM((1, vertices), jnp.int32),
            pltpu.SMEM((3, count), jnp.int32),
            pltpu.SMEM((3, count), jnp.int32),
            pltpu.VMEM((3, count, tile, tile), BF16),
            pltpu.VMEM((vertices, near_size), F32),
            pltpu.VMEM((vertices, far_size), F32),
            pltpu.SemaphoreType.DMA((4, 3)),
        ],
        size=6 << 20, name="adjacency", room=(4 << 20) + 8 * vertices * (near_size + far_size),
    )(*inputs)
    if early:
        feature_blocks[0] = near_features
    weight, known = (early[1], early[:1]) if early else (neighbor_weight, [])
    projected, message = call(
        pick, (like(width, vertices), like(border + hub, width)),
        [VM] * (3 + len(known)) + [ANY], size=1 << 20, name="pick",
    )(weight, feature_blocks[-1], choice, *known, token)
    received = swap(message, 0)
    kept = call(
        remain, like(border + hub, width), [VM] * 2, size=1 << 20, name="remain"
    )(projected, choice)
    total = call(
        own_terms, like(vertices, width, kind=F32), [VM] * (5 + len(feature_blocks)),
        flops=4 * vertices * width * (near_size + width), size=2 << 20, name="own",
    )(
        local_high, local_low, projected, near_weight, bias, *feature_blocks
    )

    keep, message, held, brief = call(
        functools.partial(step, 0, parts, cap, False, False, None),
        (like(border, width), like(border + hub, width), like(hub, width), like(border + tile, width)),
        [VM] * 4 + [ANY], name="step0",
    )(kept, kept, received, marks, total)

    def chain(level, keep, message, held, brief, marks):
        for k in range(1, steps):
            received = swap(brief if k == 1 <= level else message, k)
            last, shorten = k == steps - 1, k + 1 <= level
            outs = (
                (like(2 * border + hub, width), like(hub, width))
                if last
                else (
                    like(border, width),
                    like(border + (tile if shorten else hub), width),
                    like(hub, width),
                )
            )
            keep, message, *rest = call(
                functools.partial(step, k, parts, cap, last, k <= level, shorten),
                outs, [VM] * 4 + [ANY], name=f"step{k}_{level}",
            )(keep, held, received, marks, marks)
            held = rest[0] if rest else None
        return keep, message

    keep, message = lax.switch(
        level[0],
        [functools.partial(chain, level) for level in range(steps)],
        keep, message, held, brief, marks,
    )
    theirs = swap(message, 0)
    total = call(
        far_terms, like(vertices, width, kind=F32), [VM] * 4,
        flops=4 * vertices * width * (far_size - hub), size=2 << 20, name="far",
    )(far_high, far_low, keep, total)
    return call(finish, like(width, vertices), [VM] * 4, size=1 << 20, name="finish")(
        far_high, far_low, theirs, total
    )


def solution(mesh):
    dom, feat = P("dom"), P("feat")
    whole = P("dom", None, None)
    placed = (
        P("feat", "dom"), dom, whole, P("dom", None), P(), P(),
        dom, dom, whole, dom, dom, whole, dom, dom, whole,
        P("feat", None), P("feat", None), feat,
    )
    return jax.shard_map(
        shards, mesh=mesh, in_specs=placed, out_specs=P("feat", "dom"), check_vma=False
    )
```

```python
import functools

import jax
import jax.numpy as jnp
from jax import lax
from jax.experimental import pallas as pl
from jax.experimental.pallas import tpu as pltpu
from jax.sharding import PartitionSpec as P

BF16 = jnp.bfloat16
F32 = jnp.float32
VM = pl.BlockSpec(memory_space=pltpu.VMEM)
SM = pl.BlockSpec(memory_space=pltpu.SMEM)
ANY = pl.BlockSpec(memory_space=pl.ANY)
HBM = pl.BlockSpec(memory_space=pltpu.HBM)
LAST = (((1,), (1,)), ((), ()))
FIRST_LAST = (((0,), (1,)), ((), ()))


def call(body, outs, specs, scratch=(), flops=0, size=0, name=None, room=8 << 20):
    return pl.pallas_call(
        body,
        out_shape=outs,
        in_specs=specs,
        out_specs=jax.tree.map(lambda out: SM if out.dtype == jnp.int32 else VM, outs),
        scratch_shapes=scratch,
        compiler_params=pltpu.CompilerParams(vmem_limit_bytes=room),
        cost_estimate=pl.CostEstimate(flops=flops, bytes_accessed=size, transcendentals=0),
        name=name,
    )


def dot(a, b, contract=(((1,), (0,)), ((), ()))):
    return lax.dot_general(a, b, contract, preferred_element_type=F32)


def rows(start, size):
    return pl.ds(pl.multiple_of(start, size), size)


def line_of(place):
    for shift in (8, 4, 2, 1):
        place = place ^ (place >> shift)
    return place & 1


def order(line, bits):
    down = list(range(bits))[::-1]
    return down if line else down[-1:] + down[:-1]


def turned(chip, line, bits):
    return sum(((chip >> b) & 1) << i for i, b in enumerate(order(line, bits)))


def relative_chip(place, line, bits):
    chips = [turned(place >> 1, each, bits) for each in (0, 1)]
    return chips[0] + (chips[1] - chips[0]) * line


def relative(place, bits):
    line = line_of(place)
    return 2 * relative_chip(place, line, bits) + line


def assignments(blocks):
    if blocks != 4:
        return [[(b & 1, b >> 1) for b in range(blocks)]]
    ways = []
    for mate in (1, 2, 3):
        first = [0, mate]
        second = [b for b in range(4) if b not in first]
        for lines in ((first, second), (second, first)):
            ways.append([(int(b in lines[1]), lines[int(b in lines[1])].index(b)) for b in range(4)])
    return ways


def assign(owner, blocks, parts):
    bits = parts.bit_length() - 2
    chips = [[turned(owner[b] >> 1, line, bits) for b in range(blocks)] for line in (0, 1)]
    best = None
    for way in assignments(blocks):
        least = jnp.int32(parts - 1)
        for b in range(blocks):
            for other in range(b):
                if way[b][0] == way[other][0]:
                    apart = chips[way[b][0]][b] ^ chips[way[b][0]][other]
                    least = jnp.minimum(least, apart)
        level = sum((least >> i > 0).astype(jnp.int32) for i in range(bits))
        if best is None:
            best = level, [(jnp.int32(line), jnp.int32(slot)) for line, slot in way]
        else:
            better = level > best[0]
            best = jnp.maximum(level, best[0]), [
                (jnp.where(better, line, old), jnp.where(better, slot, place))
                for (line, slot), (old, place) in zip(way, best[1])
            ]
    return best


def partners(parts, k):
    if k == 0:
        return [(i, i ^ 1) for i in range(parts)]
    bits = parts.bit_length() - 2
    place = {relative(i, bits): i for i in range(parts)}
    return [(i, place[relative(i, bits) ^ (1 << k)]) for i in range(parts)]


def column(row):
    m = row.shape[1]
    down = lax.broadcasted_iota(jnp.int32, (m, m), 0)
    across = lax.broadcasted_iota(jnp.int32, (m, m), 1)
    return jnp.sum(jnp.where(down == across, row, jnp.zeros_like(row)), axis=1, keepdims=True)


def fetch(pairs, sems):
    copies = [pltpu.make_async_copy(a, b, sems.at[i]) for i, (a, b) in enumerate(pairs)]
    for copy in copies:
        copy.start()
    return copies


def prepare(lists_size, *refs):
    inputs, outs, scratch = refs[:18], refs[18:-13], refs[-13:]
    choice, marks, level, features, self_weight, bias = outs[:6]
    averages, parts_out = outs[6:10], outs[10:]
    owner, lists, count, hubs, weight, places, degree, dests, sources, tiles, near, far, sems = scratch
    landing = [owner, lists, count, hubs]
    landing += [ref.at[i] for i in range(3) for ref in (dests, sources, tiles)]
    landing += [degree, features, weight, self_weight, bias]
    copies = [
        pltpu.make_async_copy(a, b, sems.at[i]) for i, (a, b) in enumerate(zip(inputs, landing))
    ]
    for copy in copies:
        copy.start()
    for copy in copies[:4]:
        copy.wait()
    me = lax.axis_index("dom")
    line = line_of(me)
    parts, cap = lists.shape[1:]
    blocks, tile = hubs.shape
    vertices = choice.shape[1]
    pairs = (blocks + 1) // 2
    border, half = parts * cap // 2, parts * cap // 2 + pairs * tile
    shape = (parts, cap, cap)
    slot = lax.broadcasted_iota(jnp.int32, shape, 1)
    across = lax.broadcasted_iota(jnp.int32, shape, 2)
    index = jnp.sum(jnp.where(slot == across, lists[0][:, None, :], 0), axis=2, keepdims=True)
    shape = (parts, cap, parts)
    target = lax.broadcasted_iota(jnp.int32, shape, 0)
    across = lax.broadcasted_iota(jnp.int32, shape, 2)
    live = jnp.sum(jnp.where(target == across, count[...][None], 0), axis=2, keepdims=True)
    slot = lax.broadcasted_iota(jnp.int32, (parts, cap, 1), 1)
    index = jnp.where(slot < live, index, -1)

    def onehot(index):
        vertex = lax.broadcasted_iota(jnp.int32, (index.shape[0], vertices), 1)
        return (vertex == index).astype(F32).astype(BF16)

    for part in range(parts):
        stays = 1 - (line_of(part) ^ line)
        place = turned(part >> 1, line_of(part), parts.bit_length() - 2)
        choice[pl.ds(pl.multiple_of(stays * half + place * cap, cap), cap), :] = onehot(index[part])
    short, places_of = assign(owner, blocks, parts)
    level[0] = short
    if blocks % 2:
        odd = pl.ds(pl.multiple_of(line * half + border + (pairs - 1) * tile, cap), tile)
        choice[odd, :] = jnp.zeros((tile, vertices), BF16)
    for b, (its_line, slot) in enumerate(places_of):
        stays = 1 - (its_line ^ line)
        there = pl.ds(pl.multiple_of(stays * half + border + slot * tile, cap), tile)
        mine = jnp.where(owner[b] == me, hubs[b : b + 1, :], -1)
        choice[there, :] = onehot(column(mine))
        places[b] = lists_size + slot + (its_line ^ line) * pairs
    bits = parts.bit_length() - 2
    mine = relative(me, bits) >> 1
    marks[...] = jnp.zeros_like(marks)
    for b, (its_line, slot) in enumerate(places_of):
        owned = relative_chip(owner[b], line, bits)
        for k in range(bits):
            here = (its_line == line) & (((mine >> k) ^ 1) == (owned >> k))
            row = pl.ds(k * pairs + slot, 1)
            marks[row, :] = marks[row, :] + jnp.where(here, 1.0, 0.0)
    sum_tiles(
        copies[4:14], places, dests, sources, tiles, degree, near, far, averages
    )
    for copy in copies[14:]:
        copy.wait()
    if len(parts_out) == 2:
        known, ahead = parts_out
        width = features.shape[0]
        place = lax.axis_index("feat")
        known[...] = dot(weight[:, rows(place * width, width)], features[...])
        ahead[...] = weight[:, rows((1 - place) * width, width)]


def sum_tiles(copies, places, dests, sources, tiles, degree, near, far, averages):
    count, tile = tiles.shape[1:3]
    near[...] = jnp.zeros_like(near)
    far[...] = jnp.zeros_like(far)
    for i in range(3):
        for copy in copies[3 * i : 3 * i + 3]:
            copy.wait()
        sums = far if i else near
        for t in range(count):
            source = places[sources[i, t]] if i == 2 else sources[i, t]
            there = (rows(dests[i, t] * tile, tile), rows(source * tile, tile))
            sums[there] = sums[there] + tiles[i, t].astype(F32)
    copies[9].wait()
    for r in range(near.shape[0] // tile):
        there = slice(r * tile, (r + 1) * tile)
        below = column(degree[:, there].astype(F32))
        for sums, high, low in ((near, *averages[:2]), (far, *averages[2:])):
            mean = sums[there, :] / below
            top = mean.astype(BF16)
            high[there, :] = top
            low[there, :] = (mean - top.astype(F32)).astype(BF16)


def weight_parts(weight, feature_blocks):
    if len(feature_blocks) == 1:
        return [(weight[...], feature_blocks[0][...])]
    width = feature_blocks[0].shape[0]
    place = lax.axis_index("feat")
    return [
        (weight[:, rows(p * width, width)], block[...])
        for p, block in zip((place, 1 - place), feature_blocks)
    ]


def pick(weight, features, choice, *refs):
    *known, _, projected, message = refs
    total = dot(weight[...], features[...])
    if known:
        total = total + known[0][...]
    projected[...] = total.astype(BF16)
    message[...] = dot(
        choice[: message.shape[0], :], total.astype(BF16), LAST
    ).astype(BF16)


def remain(projected, choice, kept):
    kept[...] = dot(choice[kept.shape[0] :, :], projected[...], LAST).astype(BF16)


def step(k, parts, cap, last, short, shorten, keep, hub, received, marks, _, *outs):
    bits = parts.bit_length() - 2
    me = relative(lax.axis_index("dom"), bits)
    bit = (me >> k) & 1
    border = parts * cap // 2
    size = outs[1].shape[0] if last else outs[2].shape[0]
    held = hub[hub.shape[0] - size :, :]
    if short:
        tile = received.shape[0] - border
        arrived = received[border:, :].astype(F32)
        pairs = size // tile
        merged = jnp.concatenate(
            [
                held[i * tile : (i + 1) * tile]
                + (arrived * marks[(k - 1) * pairs + i : (k - 1) * pairs + i + 1, :]).astype(BF16)
                for i in range(pairs)
            ],
            axis=0,
        )
    else:
        merged = held + received[border:, :]
    run = (1 << k) * cap
    first, second = outs[:2]
    if last:
        for group in range(parts // 2):
            here = slice(group * cap, (group + 1) * cap)
            chips = [
                sum(((group >> (i + 1)) & 1) << b for i, b in enumerate(order(line, bits)))
                for line in (0, 1)
            ]
            for top, values in ((bit, keep), (1 - bit, received)):
                origin = jnp.where(
                    (me & 1) == 1,
                    chips[1] + (top << order(1, bits)[-1]),
                    chips[0] + (top << order(0, bits)[-1]),
                )
                place = 2 * origin + (line_of(group) ^ top)
                first[rows(place * cap, cap), :] = values[here, :]
        first[2 * border :, :] = merged
        second[...] = merged
        return
    ahead = (me >> (k + 1)) & 1
    for pair in range(parts >> (k + 2)):
        stay, go = rows((2 * pair + ahead) * run, run), rows((2 * pair + 1 - ahead) * run, run)
        mine, theirs = rows((2 * pair + bit) * run, run), rows((2 * pair + 1 - bit) * run, run)
        first[mine, :] = keep[stay, :]
        first[theirs, :] = received[stay, :]
        second[mine, :] = keep[go, :]
        second[theirs, :] = received[go, :]
    outs[2][...] = merged
    brief = outs[3] if shorten is None else second
    if shorten is None:
        second[border:, :] = merged
        brief[:border, :] = second[:border, :]
    if shorten is False:
        second[border:, :] = merged
    else:
        tile = brief.shape[0] - border
        pairs = size // tile
        brief[border:, :] = sum(merged[i * tile : (i + 1) * tile] for i in range(pairs))


def own_terms(local_high, local_low, projected, weight, bias, *refs):
    *feature_blocks, total = refs
    total[...] = (
        sum(dot(f, w, FIRST_LAST) for w, f in weight_parts(weight, feature_blocks))
        + dot(local_high[...], projected[...], LAST)
        + dot(local_low[...], projected[...], LAST)
        + bias[...]
    )


def far_terms(high, low, near, before, total):
    known = near.shape[0]
    total[...] = (
        before[...] + dot(high[:, :known], near[...]) + dot(low[:, :known], near[...])
    )


def finish(high, low, theirs, before, updated):
    known = high.shape[1] - theirs.shape[0]
    total = before[...] + dot(high[:, known:], theirs[...]) + dot(low[:, known:], theirs[...])
    updated[...] = jnp.maximum(total, 0.0).astype(BF16).T


def shards(
    features, in_degree, send_rows, send_count, hub_owner, hub_rows,
    local_dest, local_source, local_tiles, border_dest, border_source, border_tiles,
    hub_dest, hub_source, hub_tiles, self_weight, neighbor_weight, out_bias,
):
    vertices = features.shape[1]
    count, tile, _ = local_tiles.shape
    width = self_weight.shape[0]
    parts, feats = lax.axis_size("dom"), lax.axis_size("feat")
    cap = send_rows.shape[2]
    blocks = hub_owner.shape[0]
    steps = parts.bit_length() - 1
    pairs = (blocks + 1) // 2
    border, hub = parts * cap // 2, pairs * tile
    near_size, far_size = vertices, 2 * border + 2 * hub

    def like(*shape, kind=BF16):
        return jax.ShapeDtypeStruct(shape, kind)

    def swap(x, k):
        return lax.ppermute(x, "dom", partners(parts, k))

    if feats == 2:
        feature_blocks = [features, lax.ppermute(features, "feat", [(0, 1), (1, 0)])]
    else:
        feature_blocks = [lax.all_gather(features, "feat", axis=0, tiled=True)]
    fixed = [
        pltpu.with_memory_space_constraint(x, pltpu.HBM)
        for x in (
            hub_owner, send_rows, send_count, hub_rows,
            local_dest, local_source, local_tiles, border_dest, border_source, border_tiles,
            hub_dest, hub_source, hub_tiles, in_degree.reshape(1, vertices),
            features, neighbor_weight, self_weight, out_bias.reshape(1, width),
        )
    ]
    early = ()
    if feats == 2:
        early = (like(width, vertices, kind=F32), like(width, features.shape[0]))
    choice, marks, level, near_features, near_weight, bias, *averages = call(
        functools.partial(prepare, 2 * border // tile),
        (
            like(2 * (border + hub), vertices),
            like((steps - 1) * pairs, width, kind=F32),
            like(1, kind=jnp.int32),
            like(*features.shape),
            like(*self_weight.shape),
            like(1, width, kind=F32),
            *(like(vertices, near_size),) * 2,
            *(like(vertices, far_size),) * 2,
            *early,
        ),
        [HBM] * 18,
        [
            pltpu.SMEM(hub_owner.shape, jnp.int32),
            pltpu.VMEM(send_rows.shape, jnp.int32),
            pltpu.VMEM(send_count.shape, jnp.int32),
            pltpu.VMEM(hub_rows.shape, jnp.int32),
            pltpu.VMEM(neighbor_weight.shape, BF16),
            pltpu.SMEM(hub_owner.shape, jnp.int32),
            pltpu.VMEM((1, vertices), jnp.int32),
            pltpu.SMEM((3, count), jnp.int32),
            pltpu.SMEM((3, count), jnp.int32),
            pltpu.VMEM((3, count, tile, tile), BF16),
            pltpu.VMEM((vertices, near_size), F32),
            pltpu.VMEM((vertices, far_size), F32),
            pltpu.SemaphoreType.DMA((18,)),
        ],
        size=8 << 20, name="prepare", room=(8 << 20) + 8 * vertices * (near_size + far_size),
    )(*fixed)
    local_high, local_low, far_high, far_low, *early = averages
    if early:
        feature_blocks[0] = near_features
    weight, known = (early[1], early[:1]) if early else (neighbor_weight, [])
    projected, message = call(
        pick, (like(width, vertices), like(border + hub, width)),
        [VM] * (3 + len(known)) + [ANY], size=1 << 20, name="pick",
    )(weight, feature_blocks[-1], choice, *known, marks)
    received = swap(message, 0)
    kept = call(
        remain, like(border + hub, width), [VM] * 2, size=1 << 20, name="remain"
    )(projected, choice)
    own = functools.partial(call(
        own_terms, like(vertices, width, kind=F32), [VM] * (5 + len(feature_blocks)),
        flops=4 * vertices * width * (near_size + width), size=2 << 20, name="own",
    ),
        local_high, local_low, projected, near_weight, bias, *feature_blocks
    )

    keep, message, held, brief = call(
        functools.partial(step, 0, parts, cap, False, False, None),
        (like(border, width), like(border + hub, width), like(hub, width), like(border + tile, width)),
        [VM] * 4 + [ANY], name="step0",
    )(kept, kept, received, marks, marks)

    def chain(level, keep, message, held, brief, marks):
        for k in range(1, steps):
            received = swap(brief if k == 1 <= level else message, k)
            last, shorten = k == steps - 1, k + 1 <= level
            outs = (
                (like(2 * border + hub, width), like(hub, width))
                if last
                else (
                    like(border, width),
                    like(border + (tile if shorten else hub), width),
                    like(hub, width),
                )
            )
            keep, message, *rest = call(
                functools.partial(step, k, parts, cap, last, k <= level, shorten),
                outs, [VM] * 4 + [ANY], name=f"step{k}_{level}",
            )(keep, held, received, marks, marks)
            held = rest[0] if rest else None
        return keep, message

    keep, message = lax.switch(
        level[0],
        [functools.partial(chain, level) for level in range(steps)],
        keep, message, held, brief, marks,
    )
    theirs = swap(message, 0)
    total = own()
    total = call(
        far_terms, like(vertices, width, kind=F32), [VM] * 4,
        flops=4 * vertices * width * (far_size - hub), size=2 << 20, name="far",
    )(far_high, far_low, keep, total)
    return call(finish, like(width, vertices), [VM] * 4, size=1 << 20, name="finish")(
        far_high, far_low, theirs, total
    )


def solution(mesh):
    dom, feat = P("dom"), P("feat")
    whole = P("dom", None, None)
    placed = (
        P("feat", "dom"), dom, whole, P("dom", None), P(), P(),
        dom, dom, whole, dom, dom, whole, dom, dom, whole,
        P("feat", None), P("feat", None), feat,
    )
    return jax.shard_map(
        shards, mesh=mesh, in_specs=placed, out_specs=P("feat", "dom"), check_vma=False
    )
```

```python
import functools

import jax
import jax.numpy as jnp
from jax import lax
from jax.experimental import pallas as pl
from jax.experimental.pallas import tpu as pltpu
from jax.sharding import PartitionSpec as P

BF16 = jnp.bfloat16
F32 = jnp.float32
VM = pl.BlockSpec(memory_space=pltpu.VMEM)
SM = pl.BlockSpec(memory_space=pltpu.SMEM)
ANY = pl.BlockSpec(memory_space=pl.ANY)
HBM = pl.BlockSpec(memory_space=pltpu.HBM)
LAST = (((1,), (1,)), ((), ()))
FIRST_LAST = (((0,), (1,)), ((), ()))


def call(body, outs, specs, scratch=(), flops=0, size=0, name=None, room=8 << 20):
    return pl.pallas_call(
        body,
        out_shape=outs,
        in_specs=specs,
        out_specs=jax.tree.map(lambda out: SM if out.dtype == jnp.int32 else VM, outs),
        scratch_shapes=scratch,
        compiler_params=pltpu.CompilerParams(vmem_limit_bytes=room),
        cost_estimate=pl.CostEstimate(flops=flops, bytes_accessed=size, transcendentals=0),
        name=name,
    )


def dot(a, b, contract=(((1,), (0,)), ((), ()))):
    return lax.dot_general(a, b, contract, preferred_element_type=F32)


def rows(start, size):
    return pl.ds(pl.multiple_of(start, size), size)


def line_of(place):
    for shift in (8, 4, 2, 1):
        place = place ^ (place >> shift)
    return place & 1


def order(line, bits):
    down = list(range(bits))[::-1]
    return down if line else down[-1:] + down[:-1]


def turned(chip, line, bits):
    return sum(((chip >> b) & 1) << i for i, b in enumerate(order(line, bits)))


def relative_chip(place, line, bits):
    chips = [turned(place >> 1, each, bits) for each in (0, 1)]
    return chips[0] + (chips[1] - chips[0]) * line


def relative(place, bits):
    line = line_of(place)
    return 2 * relative_chip(place, line, bits) + line


def assignments(blocks):
    if blocks != 4:
        return [[(b & 1, b >> 1) for b in range(blocks)]]
    ways = []
    for mate in (1, 2, 3):
        first = [0, mate]
        second = [b for b in range(4) if b not in first]
        for lines in ((first, second), (second, first)):
            ways.append([(int(b in lines[1]), lines[int(b in lines[1])].index(b)) for b in range(4)])
    return ways


def assign(owner, blocks, parts):
    bits = parts.bit_length() - 2
    chips = [[turned(owner[b] >> 1, line, bits) for b in range(blocks)] for line in (0, 1)]
    best = None
    for way in assignments(blocks):
        least = jnp.int32(parts - 1)
        for b in range(blocks):
            for other in range(b):
                if way[b][0] == way[other][0]:
                    apart = chips[way[b][0]][b] ^ chips[way[b][0]][other]
                    least = jnp.minimum(least, apart)
        level = sum((least >> i > 0).astype(jnp.int32) for i in range(bits))
        if best is None:
            best = level, [(jnp.int32(line), jnp.int32(slot)) for line, slot in way]
        else:
            better = level > best[0]
            best = jnp.maximum(level, best[0]), [
                (jnp.where(better, line, old), jnp.where(better, slot, place))
                for (line, slot), (old, place) in zip(way, best[1])
            ]
    return best


def partners(parts, k):
    if k == 0:
        return [(i, i ^ 1) for i in range(parts)]
    bits = parts.bit_length() - 2
    place = {relative(i, bits): i for i in range(parts)}
    return [(i, place[relative(i, bits) ^ (1 << k)]) for i in range(parts)]


def column(row):
    m = row.shape[1]
    down = lax.broadcasted_iota(jnp.int32, (m, m), 0)
    across = lax.broadcasted_iota(jnp.int32, (m, m), 1)
    return jnp.sum(jnp.where(down == across, row, jnp.zeros_like(row)), axis=1, keepdims=True)


def fetch(pairs, sems):
    copies = [pltpu.make_async_copy(a, b, sems.at[i]) for i, (a, b) in enumerate(pairs)]
    for copy in copies:
        copy.start()
    return copies


def prepare(lists_size, *refs):
    inputs, outs, scratch = refs[:18], refs[18:-14], refs[-14:]
    choice, marks, level, self_weight, bias = outs[:5]
    averages, parts_out = outs[5:11], outs[11:]
    owner, lists, count, hubs, weight, features, places, degree, *rest = scratch
    dests, sources, tiles, near, far, sems = rest
    landing = [owner, lists, count, hubs]
    landing += [ref.at[i] for i in range(3) for ref in (dests, sources, tiles)]
    landing += [degree, features, weight, self_weight, bias]
    copies = [
        pltpu.make_async_copy(a, b, sems.at[i]) for i, (a, b) in enumerate(zip(inputs, landing))
    ]
    for copy in copies:
        copy.start()
    for copy in copies[:4]:
        copy.wait()
    me = lax.axis_index("dom")
    line = line_of(me)
    parts, cap = lists.shape[1:]
    blocks, tile = hubs.shape
    vertices = choice.shape[1]
    pairs = (blocks + 1) // 2
    border, half = parts * cap // 2, parts * cap // 2 + pairs * tile
    shape = (parts, cap, cap)
    slot = lax.broadcasted_iota(jnp.int32, shape, 1)
    across = lax.broadcasted_iota(jnp.int32, shape, 2)
    index = jnp.sum(jnp.where(slot == across, lists[0][:, None, :], 0), axis=2, keepdims=True)
    shape = (parts, cap, parts)
    target = lax.broadcasted_iota(jnp.int32, shape, 0)
    across = lax.broadcasted_iota(jnp.int32, shape, 2)
    live = jnp.sum(jnp.where(target == across, count[...][None], 0), axis=2, keepdims=True)
    slot = lax.broadcasted_iota(jnp.int32, (parts, cap, 1), 1)
    index = jnp.where(slot < live, index, -1)

    def onehot(index):
        vertex = lax.broadcasted_iota(jnp.int32, (index.shape[0], vertices), 1)
        return (vertex == index).astype(F32).astype(BF16)

    for part in range(parts):
        stays = 1 - (line_of(part) ^ line)
        place = turned(part >> 1, line_of(part), parts.bit_length() - 2)
        choice[pl.ds(pl.multiple_of(stays * half + place * cap, cap), cap), :] = onehot(index[part])
    short, places_of = assign(owner, blocks, parts)
    level[0] = short
    if blocks % 2:
        odd = pl.ds(pl.multiple_of(line * half + border + (pairs - 1) * tile, cap), tile)
        choice[odd, :] = jnp.zeros((tile, vertices), BF16)
    for b, (its_line, slot) in enumerate(places_of):
        stays = 1 - (its_line ^ line)
        there = pl.ds(pl.multiple_of(stays * half + border + slot * tile, cap), tile)
        mine = jnp.where(owner[b] == me, hubs[b : b + 1, :], -1)
        choice[there, :] = onehot(column(mine))
        places[b] = lists_size + slot + (its_line ^ line) * pairs
    bits = parts.bit_length() - 2
    mine = relative(me, bits) >> 1
    marks[...] = jnp.zeros_like(marks)
    for b, (its_line, slot) in enumerate(places_of):
        owned = relative_chip(owner[b], line, bits)
        for k in range(bits):
            here = (its_line == line) & (((mine >> k) ^ 1) == (owned >> k))
            row = pl.ds(k * pairs + slot, 1)
            marks[row, :] = marks[row, :] + jnp.where(here, 1.0, 0.0)
    sum_tiles(
        copies[4:14], places, dests, sources, tiles, degree, near, far, averages
    )
    for copy in copies[14:]:
        copy.wait()
    if parts_out:
        known, ahead, begun = parts_out
        width = features.shape[0]
        place = lax.axis_index("feat")
        known[...] = dot(weight[:, rows(place * width, width)], features[...])
        ahead[...] = weight[:, rows((1 - place) * width, width)]
        begun[...] = dot(self_weight[:, rows(place * width, width)], features[...]) + column(
            bias[...]
        )


def sum_tiles(copies, places, dests, sources, tiles, degree, near, far, averages):
    count, tile = tiles.shape[1:3]
    near[...] = jnp.zeros_like(near)
    far[...] = jnp.zeros_like(far)
    for i in range(3):
        for copy in copies[3 * i : 3 * i + 3]:
            copy.wait()
        sums = far if i else near
        for t in range(count):
            source = places[sources[i, t]] if i == 2 else sources[i, t]
            there = (rows(dests[i, t] * tile, tile), rows(source * tile, tile))
            sums[there] = sums[there] + tiles[i, t].astype(F32)
    copies[9].wait()
    for r in range(near.shape[0] // tile):
        there = slice(r * tile, (r + 1) * tile)
        below = column(degree[:, there].astype(F32))
        known = averages[2].shape[1]
        for sums, high, low in ((near[there, :], *averages[:2]), (far[there, :known], *averages[2:4])):
            mean = sums / below
            top = mean.astype(BF16)
            high[there, :] = top
            low[there, :] = (mean - top.astype(F32)).astype(BF16)
        mean = (far[there, known:] / below).T
        top = mean.astype(BF16)
        averages[4][:, there] = top
        averages[5][:, there] = (mean - top.astype(F32)).astype(BF16)


def pick(weight, features, choice, *refs):
    *known, _, projected, message = refs
    total = dot(weight[...], features[...])
    if known:
        total = total + known[0][...]
    projected[...] = total.astype(BF16)
    message[...] = dot(
        choice[: message.shape[0], :], total.astype(BF16), LAST
    ).astype(BF16)


def remain(projected, choice, kept):
    kept[...] = dot(choice[kept.shape[0] :, :], projected[...], LAST).astype(BF16)


def step(k, parts, cap, last, short, shorten, keep, hub, received, marks, _, *outs):
    bits = parts.bit_length() - 2
    me = relative(lax.axis_index("dom"), bits)
    bit = (me >> k) & 1
    border = parts * cap // 2
    size = outs[1].shape[0] if last else outs[2].shape[0]
    held = hub[hub.shape[0] - size :, :]
    if short:
        tile = received.shape[0] - border
        arrived = received[border:, :].astype(F32)
        pairs = size // tile
        merged = jnp.concatenate(
            [
                held[i * tile : (i + 1) * tile]
                + (arrived * marks[(k - 1) * pairs + i : (k - 1) * pairs + i + 1, :]).astype(BF16)
                for i in range(pairs)
            ],
            axis=0,
        )
    else:
        merged = held + received[border:, :]
    run = (1 << k) * cap
    first, second = outs[:2]
    if last:
        for group in range(parts // 2):
            here = slice(group * cap, (group + 1) * cap)
            chips = [
                sum(((group >> (i + 1)) & 1) << b for i, b in enumerate(order(line, bits)))
                for line in (0, 1)
            ]
            for top, values in ((bit, keep), (1 - bit, received)):
                origin = jnp.where(
                    (me & 1) == 1,
                    chips[1] + (top << order(1, bits)[-1]),
                    chips[0] + (top << order(0, bits)[-1]),
                )
                place = 2 * origin + (line_of(group) ^ top)
                first[rows(place * cap, cap), :] = values[here, :]
        first[2 * border :, :] = merged
        second[...] = merged
        return
    ahead = (me >> (k + 1)) & 1
    for pair in range(parts >> (k + 2)):
        stay, go = rows((2 * pair + ahead) * run, run), rows((2 * pair + 1 - ahead) * run, run)
        mine, theirs = rows((2 * pair + bit) * run, run), rows((2 * pair + 1 - bit) * run, run)
        first[mine, :] = keep[stay, :]
        first[theirs, :] = received[stay, :]
        second[mine, :] = keep[go, :]
        second[theirs, :] = received[go, :]
    outs[2][...] = merged
    brief = outs[3] if shorten is None else second
    if shorten is None:
        second[border:, :] = merged
        brief[:border, :] = second[:border, :]
    if shorten is False:
        second[border:, :] = merged
    else:
        tile = brief.shape[0] - border
        pairs = size // tile
        brief[border:, :] = sum(merged[i * tile : (i + 1) * tile] for i in range(pairs))


def own_terms(local_high, local_low, projected, weight, begun, features, total):
    width = features.shape[0]
    if begun.shape[0] == 1:
        rest = dot(weight[...], features[...]) + column(begun[...])
    else:
        place = lax.axis_index("feat")
        rest = begun[...] + dot(weight[:, rows((1 - place) * width, width)], features[...])
    total[...] = (
        rest
        + dot(projected[...], local_high[...], LAST)
        + dot(projected[...], local_low[...], LAST)
    )


def far_terms(high, low, near, before, total):
    total[...] = (
        before[...]
        + dot(near[...], high[...], FIRST_LAST)
        + dot(near[...], low[...], FIRST_LAST)
    )


def finish(high, low, theirs, before, updated):
    arrived = theirs[...].T
    total = before[...] + dot(arrived, high[...]) + dot(arrived, low[...])
    updated[...] = jnp.maximum(total, 0.0).astype(BF16)


def shards(
    features, in_degree, send_rows, send_count, hub_owner, hub_rows,
    local_dest, local_source, local_tiles, border_dest, border_source, border_tiles,
    hub_dest, hub_source, hub_tiles, self_weight, neighbor_weight, out_bias,
):
    vertices = features.shape[1]
    count, tile, _ = local_tiles.shape
    width = self_weight.shape[0]
    parts, feats = lax.axis_size("dom"), lax.axis_size("feat")
    cap = send_rows.shape[2]
    blocks = hub_owner.shape[0]
    steps = parts.bit_length() - 1
    pairs = (blocks + 1) // 2
    border, hub = parts * cap // 2, pairs * tile
    near_size, far_size = vertices, 2 * border + 2 * hub

    def like(*shape, kind=BF16):
        return jax.ShapeDtypeStruct(shape, kind)

    def swap(x, k):
        return lax.ppermute(x, "dom", partners(parts, k))

    if feats == 2:
        feature_blocks = [features, lax.ppermute(features, "feat", [(0, 1), (1, 0)])]
    else:
        feature_blocks = [lax.all_gather(features, "feat", axis=0, tiled=True)]
    fixed = [
        pltpu.with_memory_space_constraint(x, pltpu.HBM)
        for x in (
            hub_owner, send_rows, send_count, hub_rows,
            local_dest, local_source, local_tiles, border_dest, border_source, border_tiles,
            hub_dest, hub_source, hub_tiles, in_degree.reshape(1, vertices),
            features, neighbor_weight, self_weight, out_bias.reshape(1, width),
        )
    ]
    early = ()
    if feats == 2:
        early = (
            like(width, vertices, kind=F32),
            like(width, features.shape[0]),
            like(width, vertices, kind=F32),
        )
    choice, marks, level, near_weight, bias, *averages = call(
        functools.partial(prepare, 2 * border // tile),
        (
            like(2 * (border + hub), vertices),
            like((steps - 1) * pairs, width, kind=F32),
            like(1, kind=jnp.int32),
            like(*self_weight.shape),
            like(1, width, kind=F32),
            *(like(vertices, near_size),) * 2,
            *(like(vertices, far_size - hub),) * 2,
            *(like(hub, vertices),) * 2,
            *early,
        ),
        [HBM] * 18,
        [
            pltpu.SMEM(hub_owner.shape, jnp.int32),
            pltpu.VMEM(send_rows.shape, jnp.int32),
            pltpu.VMEM(send_count.shape, jnp.int32),
            pltpu.VMEM(hub_rows.shape, jnp.int32),
            pltpu.VMEM(neighbor_weight.shape, BF16),
            pltpu.VMEM(features.shape, BF16),
            pltpu.SMEM(hub_owner.shape, jnp.int32),
            pltpu.VMEM((1, vertices), jnp.int32),
            pltpu.SMEM((3, count), jnp.int32),
            pltpu.SMEM((3, count), jnp.int32),
            pltpu.VMEM((3, count, tile, tile), BF16),
            pltpu.VMEM((vertices, near_size), F32),
            pltpu.VMEM((vertices, far_size), F32),
            pltpu.SemaphoreType.DMA((18,)),
        ],
        size=8 << 20, name="prepare", room=(8 << 20) + 8 * vertices * (near_size + far_size),
    )(*fixed)
    local_high, local_low, far_high, far_low, late_high, late_low, *early = averages
    weight, known = (early[1], early[:1]) if early else (neighbor_weight, [])
    projected, message = call(
        pick, (like(width, vertices), like(border + hub, width)),
        [VM] * (3 + len(known)) + [ANY], size=1 << 20, name="pick",
    )(weight, feature_blocks[-1], choice, *known, marks)
    received = swap(message, 0)
    kept = call(
        remain, like(border + hub, width), [VM] * 2, size=1 << 20, name="remain"
    )(projected, choice)
    begun = early[2] if early else bias
    own = functools.partial(
        call(
            own_terms, like(width, vertices, kind=F32), [VM] * 6,
            flops=4 * vertices * width * (near_size + width), size=2 << 20, name="own",
        ),
        local_high, local_low, projected, near_weight, begun, feature_blocks[-1],
    )
    keep, message, held, brief = call(
        functools.partial(step, 0, parts, cap, False, False, None),
        (like(border, width), like(border + hub, width), like(hub, width), like(border + tile, width)),
        [VM] * 4 + [ANY], name="step0",
    )(kept, kept, received, marks, marks)

    def chain(level, keep, message, held, brief, marks):
        for k in range(1, steps):
            received = swap(brief if k == 1 <= level else message, k)
            last, shorten = k == steps - 1, k + 1 <= level
            outs = (
                (like(2 * border + hub, width), like(hub, width))
                if last
                else (
                    like(border, width),
                    like(border + (tile if shorten else hub), width),
                    like(hub, width),
                )
            )
            keep, message, *rest = call(
                functools.partial(step, k, parts, cap, last, k <= level, shorten),
                outs, [VM] * 4 + [ANY], name=f"step{k}_{level}",
            )(keep, held, received, marks, marks)
            held = rest[0] if rest else None
        return keep, message

    keep, message = lax.switch(
        level[0],
        [functools.partial(chain, level) for level in range(steps)],
        keep, message, held, brief, marks,
    )
    theirs = swap(message, 0)
    total = own()
    total = call(
        far_terms, like(width, vertices, kind=F32), [VM] * 4,
        flops=4 * vertices * width * (far_size - hub), size=2 << 20, name="far",
    )(far_high, far_low, keep, total)
    return call(finish, like(width, vertices), [VM] * 4, size=1 << 20, name="finish")(
        late_high, late_low, theirs, total
    )


def solution(mesh):
    dom, feat = P("dom"), P("feat")
    whole = P("dom", None, None)
    placed = (
        P("feat", "dom"), dom, whole, P("dom", None), P(), P(),
        dom, dom, whole, dom, dom, whole, dom, dom, whole,
        P("feat", None), P("feat", None), feat,
    )
    return jax.shard_map(
        shards, mesh=mesh, in_specs=placed, out_specs=P("feat", "dom"), check_vma=False
    )
```

```python
import functools

import jax
import jax.numpy as jnp
from jax import lax
from jax.experimental import pallas as pl
from jax.experimental.pallas import tpu as pltpu
from jax.sharding import PartitionSpec as P

BF16 = jnp.bfloat16
F32 = jnp.float32
VM = pl.BlockSpec(memory_space=pltpu.VMEM)
SM = pl.BlockSpec(memory_space=pltpu.SMEM)
ANY = pl.BlockSpec(memory_space=pl.ANY)
HBM = pl.BlockSpec(memory_space=pltpu.HBM)
LAST = (((1,), (1,)), ((), ()))
FIRST_LAST = (((0,), (1,)), ((), ()))


def call(body, outs, specs, scratch=(), flops=0, size=0, name=None, room=8 << 20):
    return pl.pallas_call(
        body,
        out_shape=outs,
        in_specs=specs,
        out_specs=jax.tree.map(lambda out: SM if out.dtype == jnp.int32 else VM, outs),
        scratch_shapes=scratch,
        compiler_params=pltpu.CompilerParams(vmem_limit_bytes=room),
        cost_estimate=pl.CostEstimate(flops=flops, bytes_accessed=size, transcendentals=0),
        name=name,
    )


def dot(a, b, contract=(((1,), (0,)), ((), ()))):
    return lax.dot_general(a, b, contract, preferred_element_type=F32)


def rows(start, size):
    return pl.ds(pl.multiple_of(start, size), size)


def line_of(place):
    for shift in (8, 4, 2, 1):
        place = place ^ (place >> shift)
    return place & 1


def order(line, bits):
    down = list(range(bits))[::-1]
    return down if line else down[-1:] + down[:-1]


def turned(chip, line, bits):
    return sum(((chip >> b) & 1) << i for i, b in enumerate(order(line, bits)))


def relative_chip(place, line, bits):
    chips = [turned(place >> 1, each, bits) for each in (0, 1)]
    return chips[0] + (chips[1] - chips[0]) * line


def relative(place, bits):
    line = line_of(place)
    return 2 * relative_chip(place, line, bits) + line


def assignments(blocks):
    if blocks != 4:
        return [[(b & 1, b >> 1) for b in range(blocks)]]
    ways = []
    for mate in (1, 2, 3):
        first = [0, mate]
        second = [b for b in range(4) if b not in first]
        for lines in ((first, second), (second, first)):
            ways.append([(int(b in lines[1]), lines[int(b in lines[1])].index(b)) for b in range(4)])
    return ways


def assign(owner, blocks, parts):
    bits = parts.bit_length() - 2
    chips = [[turned(owner[b] >> 1, line, bits) for b in range(blocks)] for line in (0, 1)]
    best = None
    for way in assignments(blocks):
        least = jnp.int32(parts - 1)
        for b in range(blocks):
            for other in range(b):
                if way[b][0] == way[other][0]:
                    apart = chips[way[b][0]][b] ^ chips[way[b][0]][other]
                    least = jnp.minimum(least, apart)
        level = sum((least >> i > 0).astype(jnp.int32) for i in range(bits))
        if best is None:
            best = level, [(jnp.int32(line), jnp.int32(slot)) for line, slot in way]
        else:
            better = level > best[0]
            best = jnp.maximum(level, best[0]), [
                (jnp.where(better, line, old), jnp.where(better, slot, place))
                for (line, slot), (old, place) in zip(way, best[1])
            ]
    return best


def partners(parts, k):
    if k == 0:
        return [(i, i ^ 1) for i in range(parts)]
    bits = parts.bit_length() - 2
    place = {relative(i, bits): i for i in range(parts)}
    return [(i, place[relative(i, bits) ^ (1 << k)]) for i in range(parts)]


def column(row):
    m = row.shape[1]
    down = lax.broadcasted_iota(jnp.int32, (m, m), 0)
    across = lax.broadcasted_iota(jnp.int32, (m, m), 1)
    return jnp.sum(jnp.where(down == across, row, jnp.zeros_like(row)), axis=1, keepdims=True)


def fetch(pairs, sems):
    copies = [pltpu.make_async_copy(a, b, sems.at[i]) for i, (a, b) in enumerate(pairs)]
    for copy in copies:
        copy.start()
    return copies


def prepare(lists_size, *refs):
    inputs, outs, scratch = refs[:18], refs[18:-14], refs[-14:]
    choice, marks, level, self_weight, bias = outs[:5]
    averages, parts_out = outs[5:11], outs[11:]
    owner, lists, count, hubs, weight, features, places, degree, *rest = scratch
    dests, sources, tiles, near, far, sems = rest
    landing = [owner, lists, count, hubs]
    landing += [ref.at[i] for i in range(3) for ref in (dests, sources, tiles)]
    landing += [degree, features, weight, self_weight, bias]
    copies = [
        pltpu.make_async_copy(a, b, sems.at[i]) for i, (a, b) in enumerate(zip(inputs, landing))
    ]
    for copy in copies:
        copy.start()
    for copy in copies[:4]:
        copy.wait()
    me = lax.axis_index("dom")
    line = line_of(me)
    parts, cap = lists.shape[1:]
    blocks, tile = hubs.shape
    vertices = choice.shape[1]
    pairs = (blocks + 1) // 2
    border, half = parts * cap // 2, parts * cap // 2 + pairs * tile
    shape = (parts, cap, cap)
    slot = lax.broadcasted_iota(jnp.int32, shape, 1)
    across = lax.broadcasted_iota(jnp.int32, shape, 2)
    index = jnp.sum(jnp.where(slot == across, lists[0][:, None, :], 0), axis=2, keepdims=True)
    shape = (parts, cap, parts)
    target = lax.broadcasted_iota(jnp.int32, shape, 0)
    across = lax.broadcasted_iota(jnp.int32, shape, 2)
    live = jnp.sum(jnp.where(target == across, count[...][None], 0), axis=2, keepdims=True)
    slot = lax.broadcasted_iota(jnp.int32, (parts, cap, 1), 1)
    index = jnp.where(slot < live, index, -1)

    def onehot(index):
        vertex = lax.broadcasted_iota(jnp.int32, (index.shape[0], vertices), 1)
        return (vertex == index).astype(F32).astype(BF16)

    for part in range(parts):
        stays = 1 - (line_of(part) ^ line)
        place = turned(part >> 1, line_of(part), parts.bit_length() - 2)
        choice[pl.ds(pl.multiple_of(stays * half + place * cap, cap), cap), :] = onehot(index[part])
    short, places_of = assign(owner, blocks, parts)
    level[0] = short
    if blocks % 2:
        odd = pl.ds(pl.multiple_of(line * half + border + (pairs - 1) * tile, cap), tile)
        choice[odd, :] = jnp.zeros((tile, vertices), BF16)
    for b, (its_line, slot) in enumerate(places_of):
        stays = 1 - (its_line ^ line)
        there = pl.ds(pl.multiple_of(stays * half + border + slot * tile, cap), tile)
        mine = jnp.where(owner[b] == me, hubs[b : b + 1, :], -1)
        choice[there, :] = onehot(column(mine))
        places[b] = lists_size + slot + (its_line ^ line) * pairs
    bits = parts.bit_length() - 2
    mine = relative(me, bits) >> 1
    marks[...] = jnp.zeros_like(marks)
    for b, (its_line, slot) in enumerate(places_of):
        owned = relative_chip(owner[b], line, bits)
        for k in range(bits):
            here = (its_line == line) & (((mine >> k) ^ 1) == (owned >> k))
            row = pl.ds(k * pairs + slot, 1)
            marks[row, :] = marks[row, :] + jnp.where(here, 1.0, 0.0)
    sum_tiles(
        copies[4:14], places, dests, sources, tiles, degree, near, far, averages
    )
    for copy in copies[14:]:
        copy.wait()
    if parts_out:
        known, ahead, begun = parts_out
        width = features.shape[0]
        place = lax.axis_index("feat")
        known[...] = dot(weight[:, rows(place * width, width)], features[...])
        ahead[...] = weight[:, rows((1 - place) * width, width)]
        begun[...] = dot(self_weight[:, rows(place * width, width)], features[...]) + column(
            bias[...]
        )


def sum_tiles(copies, places, dests, sources, tiles, degree, near, far, averages):
    count, tile = tiles.shape[1:3]
    near[...] = jnp.zeros_like(near)
    far[...] = jnp.zeros_like(far)
    for i in range(3):
        for copy in copies[3 * i : 3 * i + 3]:
            copy.wait()
        sums = far if i else near
        for t in range(count):
            source = places[sources[i, t]] if i == 2 else sources[i, t]
            there = (rows(dests[i, t] * tile, tile), rows(source * tile, tile))
            sums[there] = sums[there] + tiles[i, t].astype(F32)
    copies[9].wait()
    for r in range(near.shape[0] // tile):
        there = slice(r * tile, (r + 1) * tile)
        below = column(degree[:, there].astype(F32))
        known = averages[2].shape[1]
        for sums, high, low in ((near[there, :], *averages[:2]), (far[there, :known], *averages[2:4])):
            mean = sums / below
            top = mean.astype(BF16)
            high[there, :] = top
            low[there, :] = (mean - top.astype(F32)).astype(BF16)
        mean = (far[there, known:] / below).T
        top = mean.astype(BF16)
        averages[4][:, there] = top
        averages[5][:, there] = (mean - top.astype(F32)).astype(BF16)


def pick(weight, features, choice, *refs):
    *known, _, projected, message = refs
    total = dot(weight[...], features[...])
    if known:
        total = total + known[0][...]
    projected[...] = total.astype(BF16)
    message[...] = dot(
        choice[: message.shape[0], :], total.astype(BF16), LAST
    ).astype(BF16)


def remain(projected, choice, kept):
    kept[...] = dot(choice[kept.shape[0] :, :], projected[...], LAST).astype(BF16)


def step(k, parts, cap, last, short, shorten, keep, hub, received, marks, _, *outs):
    bits = parts.bit_length() - 2
    me = relative(lax.axis_index("dom"), bits)
    bit = (me >> k) & 1
    border = parts * cap // 2
    size = outs[1].shape[0] if last else outs[2].shape[0]
    held = hub[hub.shape[0] - size :, :]
    if short:
        tile = received.shape[0] - border
        arrived = received[border:, :].astype(F32)
        pairs = size // tile
        merged = jnp.concatenate(
            [
                held[i * tile : (i + 1) * tile]
                + (arrived * marks[(k - 1) * pairs + i : (k - 1) * pairs + i + 1, :]).astype(BF16)
                for i in range(pairs)
            ],
            axis=0,
        )
    else:
        merged = held + received[border:, :]
    run = (1 << k) * cap
    first, second = outs[:2]
    if last:
        for group in range(parts // 2):
            here = slice(group * cap, (group + 1) * cap)
            chips = [
                sum(((group >> (i + 1)) & 1) << b for i, b in enumerate(order(line, bits)))
                for line in (0, 1)
            ]
            for top, values in ((bit, keep), (1 - bit, received)):
                origin = jnp.where(
                    (me & 1) == 1,
                    chips[1] + (top << order(1, bits)[-1]),
                    chips[0] + (top << order(0, bits)[-1]),
                )
                place = 2 * origin + (line_of(group) ^ top)
                first[rows(place * cap, cap), :] = values[here, :]
        first[2 * border :, :] = merged
        second[...] = merged
        return
    ahead = (me >> (k + 1)) & 1
    for pair in range(parts >> (k + 2)):
        stay, go = rows((2 * pair + ahead) * run, run), rows((2 * pair + 1 - ahead) * run, run)
        mine, theirs = rows((2 * pair + bit) * run, run), rows((2 * pair + 1 - bit) * run, run)
        first[mine, :] = keep[stay, :]
        first[theirs, :] = received[stay, :]
        second[mine, :] = keep[go, :]
        second[theirs, :] = received[go, :]
    outs[2][...] = merged
    brief = outs[3] if shorten is None else second
    if shorten is None:
        second[border:, :] = merged
        brief[:border, :] = second[:border, :]
    if shorten is False:
        second[border:, :] = merged
    else:
        tile = brief.shape[0] - border
        pairs = size // tile
        brief[border:, :] = sum(merged[i * tile : (i + 1) * tile] for i in range(pairs))


def known_terms(
    local_high, local_low, projected, weight, begun, features, high, low, near, total
):
    width = features.shape[0]
    if begun.shape[0] == 1:
        rest = dot(weight[...], features[...]) + column(begun[...])
    else:
        place = lax.axis_index("feat")
        rest = begun[...] + dot(weight[:, rows((1 - place) * width, width)], features[...])
    total[...] = (
        rest
        + dot(projected[...], local_high[...], LAST)
        + dot(projected[...], local_low[...], LAST)
        + dot(near[...], high[...], FIRST_LAST)
        + dot(near[...], low[...], FIRST_LAST)
    )


def finish(high, low, theirs, before, updated):
    arrived = theirs[...].T
    total = before[...] + dot(arrived, high[...]) + dot(arrived, low[...])
    updated[...] = jnp.maximum(total, 0.0).astype(BF16)


def shards(
    features, in_degree, send_rows, send_count, hub_owner, hub_rows,
    local_dest, local_source, local_tiles, border_dest, border_source, border_tiles,
    hub_dest, hub_source, hub_tiles, self_weight, neighbor_weight, out_bias,
):
    vertices = features.shape[1]
    count, tile, _ = local_tiles.shape
    width = self_weight.shape[0]
    parts, feats = lax.axis_size("dom"), lax.axis_size("feat")
    cap = send_rows.shape[2]
    blocks = hub_owner.shape[0]
    steps = parts.bit_length() - 1
    pairs = (blocks + 1) // 2
    border, hub = parts * cap // 2, pairs * tile
    near_size, far_size = vertices, 2 * border + 2 * hub

    def like(*shape, kind=BF16):
        return jax.ShapeDtypeStruct(shape, kind)

    def swap(x, k):
        return lax.ppermute(x, "dom", partners(parts, k))

    if feats == 2:
        feature_blocks = [features, lax.ppermute(features, "feat", [(0, 1), (1, 0)])]
    else:
        feature_blocks = [lax.all_gather(features, "feat", axis=0, tiled=True)]
    fixed = [
        pltpu.with_memory_space_constraint(x, pltpu.HBM)
        for x in (
            hub_owner, send_rows, send_count, hub_rows,
            local_dest, local_source, local_tiles, border_dest, border_source, border_tiles,
            hub_dest, hub_source, hub_tiles, in_degree.reshape(1, vertices),
            features, neighbor_weight, self_weight, out_bias.reshape(1, width),
        )
    ]
    early = ()
    if feats == 2:
        early = (
            like(width, vertices, kind=F32),
            like(width, features.shape[0]),
            like(width, vertices, kind=F32),
        )
    choice, marks, level, near_weight, bias, *averages = call(
        functools.partial(prepare, 2 * border // tile),
        (
            like(2 * (border + hub), vertices),
            like((steps - 1) * pairs, width, kind=F32),
            like(1, kind=jnp.int32),
            like(*self_weight.shape),
            like(1, width, kind=F32),
            *(like(vertices, near_size),) * 2,
            *(like(vertices, far_size - hub),) * 2,
            *(like(hub, vertices),) * 2,
            *early,
        ),
        [HBM] * 18,
        [
            pltpu.SMEM(hub_owner.shape, jnp.int32),
            pltpu.VMEM(send_rows.shape, jnp.int32),
            pltpu.VMEM(send_count.shape, jnp.int32),
            pltpu.VMEM(hub_rows.shape, jnp.int32),
            pltpu.VMEM(neighbor_weight.shape, BF16),
            pltpu.VMEM(features.shape, BF16),
            pltpu.SMEM(hub_owner.shape, jnp.int32),
            pltpu.VMEM((1, vertices), jnp.int32),
            pltpu.SMEM((3, count), jnp.int32),
            pltpu.SMEM((3, count), jnp.int32),
            pltpu.VMEM((3, count, tile, tile), BF16),
            pltpu.VMEM((vertices, near_size), F32),
            pltpu.VMEM((vertices, far_size), F32),
            pltpu.SemaphoreType.DMA((18,)),
        ],
        size=8 << 20, name="prepare", room=(8 << 20) + 8 * vertices * (near_size + far_size),
    )(*fixed)
    local_high, local_low, far_high, far_low, late_high, late_low, *early = averages
    weight, known = (early[1], early[:1]) if early else (neighbor_weight, [])
    projected, message = call(
        pick, (like(width, vertices), like(border + hub, width)),
        [VM] * (3 + len(known)) + [ANY], size=1 << 20, name="pick",
    )(weight, feature_blocks[-1], choice, *known, marks)
    received = swap(message, 0)
    kept = call(
        remain, like(border + hub, width), [VM] * 2, size=1 << 20, name="remain"
    )(projected, choice)
    begun = early[2] if early else bias
    keep, message, held, brief = call(
        functools.partial(step, 0, parts, cap, False, False, None),
        (like(border, width), like(border + hub, width), like(hub, width), like(border + tile, width)),
        [VM] * 4 + [ANY], name="step0",
    )(kept, kept, received, marks, marks)

    def chain(level, keep, message, held, brief, marks):
        for k in range(1, steps):
            received = swap(brief if k == 1 <= level else message, k)
            last, shorten = k == steps - 1, k + 1 <= level
            outs = (
                (like(2 * border + hub, width), like(hub, width))
                if last
                else (
                    like(border, width),
                    like(border + (tile if shorten else hub), width),
                    like(hub, width),
                )
            )
            keep, message, *rest = call(
                functools.partial(step, k, parts, cap, last, k <= level, shorten),
                outs, [VM] * 4 + [ANY], name=f"step{k}_{level}",
            )(keep, held, received, marks, marks)
            held = rest[0] if rest else None
        return keep, message

    keep, message = lax.switch(
        level[0],
        [functools.partial(chain, level) for level in range(steps)],
        keep, message, held, brief, marks,
    )
    theirs = swap(message, 0)
    total = call(
        known_terms, like(width, vertices, kind=F32), [VM] * 9,
        flops=4 * vertices * width * (near_size + far_size), size=4 << 20, name="known",
    )(
        local_high, local_low, projected, near_weight, early[2] if early else bias,
        feature_blocks[-1], far_high, far_low, keep,
    )
    return call(finish, like(width, vertices), [VM] * 4, size=1 << 20, name="finish")(
        late_high, late_low, theirs, total
    )


def solution(mesh):
    dom, feat = P("dom"), P("feat")
    whole = P("dom", None, None)
    placed = (
        P("feat", "dom"), dom, whole, P("dom", None), P(), P(),
        dom, dom, whole, dom, dom, whole, dom, dom, whole,
        P("feat", None), P("feat", None), feat,
    )
    return jax.shard_map(
        shards, mesh=mesh, in_specs=placed, out_specs=P("feat", "dom"), check_vma=False
    )
```
